768 devices in a mesh: tm: 32 (over x, z_hi, core), dp: 24 (over z_lo, y).
Axes of the slice: x: 4, y: 8, z: 12 (z_hi: 4, z_lo: 3; z = z_hi * 3 + z_lo), core: 2. Of those that a mesh axis runs over, the one named last changes fastest.
Arguments:
- frames_in: bfloat16 [24, 4096, 1024], P('dp', 'tm'), may hold values from -6 to 6
- valid_frames: int32 [24], P('dp'), may hold values from 2048 to 4096, as said below
- kernel: float32 [9, 1024], replicated, may hold values from -2 to 2
- w_qkv: bfloat16 [1024, 3072], replicated, may hold values from -0.1875 to 0.1875
- cotangent: bfloat16 [24, 4096, 1024], P('dp', 'tm'), may hold values from -6 to 6
Outputs:
- attended: bfloat16 [24, 4096, 1024], P('dp', 'tm')
- grad_in: bfloat16 [24, 4096, 1024], P('dp', 'tm')
- qkv_grad: float32 [24, 128, 1024], P('dp', None, 'tm')
The draws below stay inside these ranges and needn't reach their ends.
Inputs may be any that keep to these rules, and one draw needn't show every extreme that they name: `valid_frames`: valid frames of each recording, counted from its start; some recording has all 4096 and some exactly 2048.
All inputs are finite; a program needn't handle non-finite values.
Results may differ from the reference program's by a relative error of at most 0.025.
Values may be sent and summed in bfloat16 or wider, within the bound.
A program may use at most 64 MiB of HBM per device.

```python
import jax
import jax.numpy as jnp
from jax import lax

D = 1024
HEADS = 8
HEAD = 128
KERNEL = 9
LEFT = 70
F_DEV = 128
FRAMES = 4096
RECS = 24


def draw_valid_frames(key, part):
    first, second = jax.random.split(jax.random.fold_in(key, 11))
    counts = jax.random.randint(first, (RECS,), FRAMES // 2, FRAMES + 1)
    order = jax.random.permutation(second, RECS)
    places = jnp.arange(RECS)
    counts = jnp.where(places == order[0], FRAMES, counts)
    counts = jnp.where(places == order[1], FRAMES // 2, counts)
    return counts.astype(jnp.int32)


def strengthened(array, stream_key, source, target, parts, factor):
    owner, partner = [(jnp.arange(array.shape[axis_at]) // (array.shape[axis_at] // parts)).reshape([-1 if axis == axis_at else 1 for axis in range(array.ndim)]) for axis_at in (source, target)]
    chosen = jax.random.permutation(stream_key, parts)[partner]
    strong = (owner == chosen) | (owner == (partner + parts // 2) % parts)
    return jnp.where(strong, factor * array, array)


def steps_of(key, dims, cuts, smallest, high):
    loudness = 1.0
    for dim, shards_of in cuts:
        heights = jax.random.uniform(jax.random.fold_in(jax.random.fold_in(key, 6), dim), (shards_of,), jnp.float32, smallest / len(cuts), high / len(cuts))
        loudness = loudness * jnp.repeat(jnp.exp(heights), dims[dim] // shards_of).reshape((-1,) + (1,) * (len(dims) - 1 - dim))
    return loudness


def noise(key, dims, scale, bound, cuts=(), kind=jnp.bfloat16):
    gain = steps_of(key, dims, cuts, -0.22, 0.18) if cuts else 1.0
    drawn = jax.random.normal(key, dims, jnp.float32) * scale * gain
    return jnp.minimum(jnp.maximum(drawn, -bound), bound).astype(kind)


def heavy_noise(rng, shape, width, bound, pieces, heavy, held_as=jnp.bfloat16):
    array = width * jax.random.normal(rng, shape, jnp.float32)
    if pieces:
        array = array * steps_of(rng, shape, pieces, -0.22, 0.18)
    return jnp.clip(strengthened(array, jax.random.fold_in(rng, 3), *heavy), -bound, bound).astype(held_as)


def setup_inputs(seed: int = 0) -> dict:
    splits = jax.random.split(jax.random.key(seed), 6)
    frames_in = heavy_noise(splits[0], (RECS, FRAMES, D), 1.0, 6.0, ((0, 24), (1, 32)), (1, 2, 32, 2.75))
    valid_frames = draw_valid_frames(jax.random.fold_in(splits[5], 71), 0)
    kernel = noise(splits[2], (KERNEL, D), KERNEL ** -0.5, 2.0, (), jnp.float32)
    w_qkv = noise(splits[3], (D, 3 * D), D ** -0.5, 0.1875)
    cotangent = noise(splits[4], (RECS, FRAMES, D), 1.0, 6.0, ((0, 24), (1, 32)))
    return {"frames_in": frames_in, "valid_frames": valid_frames, "kernel": kernel, "w_qkv": w_qkv, "cotangent": cotangent}


def conv_rows(extended, taps, count):
    total = jnp.zeros((count, extended.shape[1]), jnp.float32)
    for offset in range(KERNEL):
        total = total + taps[offset] * extended[offset:offset + count]
    return total


def band_pass(queries, keys_ext, vals_ext, grad_out, query_pos, key_pos, count):
    factor = HEAD ** -0.5
    offset = query_pos[:, None] - key_pos[None, :]
    allowed = (offset >= 0) & (offset <= LEFT) & (key_pos[None, :] >= 0) & (key_pos[None, :] < count) & (query_pos[:, None] < count)
    q_heads = queries.astype(jnp.float32).reshape(-1, HEADS, HEAD)
    k_heads = keys_ext.astype(jnp.float32).reshape(-1, HEADS, HEAD)
    v_heads = vals_ext.astype(jnp.float32).reshape(-1, HEADS, HEAD)
    g_heads = grad_out.astype(jnp.float32).reshape(-1, HEADS, HEAD)
    scores = jnp.einsum("fhe,ghe->hfg", q_heads, k_heads) * factor
    raised = jnp.where(allowed[None], jnp.exp(scores), 0.0)
    missing = 1.0 - (query_pos < count).astype(jnp.float32)
    prob = raised / (jnp.sum(raised, axis=-1, keepdims=True) + missing[None, :, None])
    prob_low = prob.astype(jnp.bfloat16)
    attended = jnp.einsum("hfg,ghe->fhe", prob_low.astype(jnp.float32), v_heads)
    attended = attended.reshape(queries.shape).astype(jnp.bfloat16)
    grad_prob = jnp.einsum("fhe,ghe->hfg", g_heads, v_heads)
    grad_score = (prob * (grad_prob - jnp.sum(prob * grad_prob, axis=-1, keepdims=True)) * factor).astype(jnp.bfloat16)
    grad_query = jnp.einsum("hfg,ghe->fhe", grad_score.astype(jnp.float32), k_heads).reshape(queries.shape)
    grad_key = jnp.einsum("hfg,fhe->ghe", grad_score.astype(jnp.float32), q_heads).reshape(keys_ext.shape)
    grad_value = jnp.einsum("hfg,fhe->ghe", prob_low.astype(jnp.float32), g_heads).reshape(vals_ext.shape)
    return attended, grad_query, grad_key, grad_value


def reference(frames_in, valid_frames, kernel, w_qkv, cotangent):
    blocks = FRAMES // F_DEV
    factor = float(RECS * FRAMES) ** -0.5

    def one_recording(total, item):
        record, count, cot_rec = item
        positions = jnp.arange(FRAMES, dtype=jnp.int32)
        live = (positions < count)[:, None]
        masked = jnp.where(live, record, jnp.zeros_like(record))
        padded = jnp.concatenate([jnp.zeros((KERNEL - 1, D), jnp.float32), masked.astype(jnp.float32)], axis=0)
        conv = conv_rows(padded, kernel, FRAMES)
        hidden = (masked.astype(jnp.float32) + jax.nn.silu(conv)).astype(jnp.bfloat16)
        qkv = jnp.dot(hidden, w_qkv, preferred_element_type=jnp.float32).astype(jnp.bfloat16)
        grad_out = jnp.where(live, cot_rec, jnp.zeros_like(cot_rec))
        kv_pad = jnp.concatenate([jnp.zeros((LEFT, 2 * D), jnp.bfloat16), qkv[:, D:]], axis=0)

        def one_block(index):
            begin = index * F_DEV
            queries = lax.dynamic_slice_in_dim(qkv[:, :D], begin, F_DEV, 0)
            pairs = lax.dynamic_slice_in_dim(kv_pad, begin, F_DEV + LEFT, 0)
            grads = lax.dynamic_slice_in_dim(grad_out, begin, F_DEV, 0)
            query_pos = begin + jnp.arange(F_DEV, dtype=jnp.int32)
            key_pos = begin - LEFT + jnp.arange(F_DEV + LEFT, dtype=jnp.int32)
            return band_pass(queries, pairs[:, :D], pairs[:, D:], grads, query_pos, key_pos, count)

        attended, grad_query, grad_key, grad_value = lax.map(one_block, jnp.arange(blocks, dtype=jnp.int32))
        zero_rim = jnp.zeros((1, LEFT, D), jnp.float32)
        later_key = jnp.concatenate([grad_key[1:, :LEFT], zero_rim], axis=0)
        later_value = jnp.concatenate([grad_value[1:, :LEFT], zero_rim], axis=0)
        own_key = grad_key[:, LEFT:]
        own_value = grad_value[:, LEFT:]
        own_key = jnp.concatenate([own_key[:, :F_DEV - LEFT], own_key[:, F_DEV - LEFT:] + later_key], axis=1)
        own_value = jnp.concatenate([own_value[:, :F_DEV - LEFT], own_value[:, F_DEV - LEFT:] + later_value], axis=1)
        grad_qkv = jnp.concatenate([grad_query, own_key, own_value], axis=-1).reshape(FRAMES, 3 * D).astype(jnp.bfloat16)
        grad_hidden = lax.dot_general(grad_qkv, w_qkv, (((1,), (1,)), ((), ())), preferred_element_type=jnp.float32)
        logistic = jax.nn.sigmoid(conv)
        grad_conv = grad_hidden * logistic * (1.0 + conv * (1.0 - logistic))
        tail = jnp.concatenate([grad_conv, jnp.zeros((KERNEL - 1, D), jnp.float32)], axis=0)
        spread = conv_rows(tail, kernel[::-1], FRAMES)
        grad_in = jnp.where(live, grad_hidden + spread, 0.0).astype(jnp.bfloat16)
        hidden_blocks = hidden.reshape(blocks, F_DEV, D)
        grad_blocks = grad_qkv.reshape(blocks, F_DEV, 3 * D)

        def add_block(running, pair):
            term = lax.dot_general(pair[0], pair[1], (((0,), (0,)), ((), ())), preferred_element_type=jnp.float32)
            rounded = lax.optimization_barrier(term.astype(jnp.bfloat16))
            return running + rounded.astype(jnp.float32), None

        total, _ = lax.scan(add_block, total, (hidden_blocks, grad_blocks))
        return total, (attended.reshape(FRAMES, D), grad_in)

    start = jnp.zeros((D, 3 * D), jnp.float32)
    total, outputs = lax.scan(one_recording, start, (frames_in, valid_frames, cotangent))
    qkv_grad = (total * factor).reshape(D, 3 * HEADS, HEAD).transpose(1, 2, 0)
    return outputs[0], outputs[1], qkv_grad
```

```python
import functools

import jax
import jax.numpy as jnp
from jax import lax
from jax.experimental import pallas as pl
from jax.experimental.pallas import tpu as pltpu
from jax.sharding import PartitionSpec as P

HEADS = 8
HEAD = 128
KERNEL = 9
LEFT = 70
HALO = 80
FRAMES = 128
WIDTH = 1024
EXT = HALO + FRAMES + HALO
AHEAD = FRAMES + HALO
GROWS = FRAMES + 16
PAIR = 2 * HEAD
SECTION = 3 * PAIR

NX, NY, NZ, NZ_LO = 4, 8, 12, 3
MESH = pl.DeviceIdType.MESH


def dot_nn(a, b):
    return lax.dot_general(a, b, (((1,), (0,)), ((), ())), preferred_element_type=jnp.float32)


def dot_nt(a, b):
    return lax.dot_general(a, b, (((1,), (1,)), ((), ())), preferred_element_type=jnp.float32)


def dot_tn(a, b):
    return lax.dot_general(a, b, (((0,), (0,)), ((), ())), preferred_element_type=jnp.float32)


def halo_kernel(x_ref, c_ref, xp_ref, xn_ref, cn_ref, send, recv):
    count = lax.axis_size("tm")
    me = lax.axis_index("tm")
    after, before = lax.rem(me + 1, count), lax.rem(me + count - 1, count)
    barrier = pltpu.get_barrier_semaphore()
    for other in (before, after):
        pl.semaphore_signal(barrier, inc=1, device_id={"tm": other}, device_id_type=MESH)
    pl.semaphore_wait(barrier, 2)

    def copy(source, target, slot, other):
        return pltpu.make_async_remote_copy(
            src_ref=source,
            dst_ref=target,
            send_sem=send.at[slot],
            recv_sem=recv.at[slot],
            device_id={"tm": other},
            device_id_type=MESH,
        )

    copies = [
        copy(x_ref.at[0, pl.ds(FRAMES - HALO, HALO)], xp_ref, 0, after),
        copy(x_ref.at[0, pl.ds(0, HALO)], xn_ref, 1, before),
        copy(c_ref.at[0, pl.ds(0, HALO)], cn_ref, 2, before),
    ]
    for one in copies:
        one.start()
    for one in copies:
        one.wait()


def exchange_halo(frames_in, cotangent):
    shape = jax.ShapeDtypeStruct((HALO, WIDTH), jnp.bfloat16)
    anywhere = pl.BlockSpec(memory_space=pl.ANY)
    return pl.pallas_call(
        halo_kernel,
        out_shape=(shape, shape, shape),
        in_specs=[anywhere, anywhere],
        out_specs=(anywhere, anywhere, anywhere),
        scratch_shapes=[pltpu.SemaphoreType.DMA((3,)), pltpu.SemaphoreType.DMA((3,))],
        compiler_params=pltpu.CompilerParams(collective_id=0, has_side_effects=True),
        name="halo",
    )(frames_in, cotangent)


def compute_kernel(
    where_ref, x_ref, xp_ref, xn_ref, c_ref, cn_ref, taps_ref, w_ref,
    att_ref, gin_ref, ht_ref, g_ref,
    ext, hid, slope, cot, mask_own, mask_next, qkv, gq, gh, gc, wbuf, wsem,
):
    begin, count = where_ref[0], where_ref[1]
    factor = HEAD ** (-0.5)

    def weight(pair, section):
        return pltpu.make_async_copy(
            w_ref.at[:, pl.ds(section * WIDTH + pair * PAIR, PAIR)],
            wbuf.at[pair, :, pl.ds(section * PAIR, PAIR)],
            wsem.at[pair, section],
        )

    for pair in range(HEADS // 2):
        for section in range(3):
            weight(pair, section).start()

    def live_rows(first, rows):
        at = first + lax.broadcasted_iota(jnp.int32, (rows, 1), 0)
        return (at >= 0) & (at < count)

    def fill(row, first, ref, rows):
        value = ref.astype(jnp.float32)
        ext[row : row + rows, :] = jnp.where(live_rows(first, rows), value, 0.0)

    ext[0:8, :] = jnp.zeros((8, WIDTH), jnp.float32)
    fill(8, begin - HALO, xp_ref[...], HALO)
    fill(8 + HALO, begin, x_ref[0], FRAMES)
    fill(8 + HALO + FRAMES, begin + FRAMES, xn_ref[...], HALO)
    cot[0:FRAMES, :] = jnp.where(live_rows(begin, FRAMES), c_ref[0].astype(jnp.float32), 0.0).astype(jnp.bfloat16)
    cot[FRAMES:AHEAD, :] = jnp.where(
        live_rows(begin + FRAMES, HALO), cn_ref[...].astype(jnp.float32), 0.0
    ).astype(jnp.bfloat16)

    def band(rows, columns, first_query, first_key):
        query = first_query + lax.broadcasted_iota(jnp.int32, (rows, columns), 0)
        key = first_key + lax.broadcasted_iota(jnp.int32, (rows, columns), 1)
        offset = query - key
        allowed = (offset >= 0) & (offset <= LEFT) & (key >= 0) & (key < count) & (query < count)
        return jnp.where(allowed, 1.0, 0.0)

    mask_own[...] = band(FRAMES, AHEAD, begin, begin - HALO)
    mask_next[...] = band(HALO, 2 * HALO, begin + FRAMES, begin + FRAMES - HALO)

    def conv_rows(step, _):
        row = pl.multiple_of(step * 16, 16)
        window = ext[pl.ds(row, 24), :]
        total = jnp.zeros((16, WIDTH), jnp.float32)
        for tap in range(KERNEL):
            total = total + taps_ref[tap : tap + 1, :] * window[tap : tap + 16]
        logistic = 1.0 / (1.0 + jnp.exp(-total))
        hid[pl.ds(row, 16), :] = (window[8:24] + total * logistic).astype(jnp.bfloat16)
        slope[pl.ds(row, 16), :] = logistic * (1.0 + total * (1.0 - logistic))
        return 0

    lax.fori_loop(0, EXT // 16, conv_rows, 0)

    for block in range(WIDTH // 128):
        tile = hid[HALO : HALO + FRAMES, block * 128 : (block + 1) * 128]
        turned = tile.astype(jnp.float32).T.astype(jnp.bfloat16)
        for piece in range(8):
            group = block * 2 + piece // 4
            ht_ref[(piece // 2) % 2, piece % 2, group * 16 : (group + 1) * 16, :] = turned[
                piece * 16 : (piece + 1) * 16
            ]

    gh[...] = jnp.zeros_like(gh)

    def attend(q, g, k, v, mask, first):
        raised = jnp.where(mask > 0.5, jnp.exp(dot_nt(q, k) * factor), 0.0)
        at = first + lax.broadcasted_iota(jnp.int32, (q.shape[0], 1), 0)
        missing = jnp.where(at < count, 0.0, 1.0)
        prob = raised * (1.0 / (jnp.sum(raised, axis=1, keepdims=True) + missing))
        grad_prob = dot_nt(g, v)
        mean = jnp.sum(prob * grad_prob, axis=1, keepdims=True)
        grad_score = (prob * (grad_prob - mean) * factor).astype(jnp.bfloat16)
        return prob.astype(jnp.bfloat16), grad_score

    def two_heads(pair, _):
        for section in range(3):
            weight(pair, section).wait()
        w = wbuf[pair]
        qkv[...] = dot_nn(hid[...], w).astype(jnp.bfloat16)
        for head in range(2):
            column = pl.multiple_of(pair * PAIR + head * HEAD, HEAD)
            q_at, k_at, v_at = (section * PAIR + head * HEAD for section in range(3))
            q_own = qkv[HALO : HALO + FRAMES, q_at : q_at + HEAD]
            q_next = qkv[HALO + FRAMES : EXT, q_at : q_at + HEAD]
            k_own = qkv[0:AHEAD, k_at : k_at + HEAD]
            k_next = qkv[FRAMES:EXT, k_at : k_at + HEAD]
            v_own = qkv[0:AHEAD, v_at : v_at + HEAD]
            v_next = qkv[FRAMES:EXT, v_at : v_at + HEAD]
            g_own = cot[0:FRAMES, pl.ds(column, HEAD)]
            g_next = cot[FRAMES:AHEAD, pl.ds(column, HEAD)]
            prob_own, score_own = attend(q_own, g_own, k_own, v_own, mask_own[...], begin)
            prob_next, score_next = attend(
                q_next, g_next, k_next, v_next, mask_next[...], begin + FRAMES
            )
            att_ref[0, :, pl.ds(column, HEAD)] = dot_nn(prob_own, v_own).astype(jnp.bfloat16)
            gq[0:FRAMES, q_at : q_at + HEAD] = dot_nn(score_own, k_own).astype(jnp.bfloat16)
            gq[FRAMES:GROWS, q_at : q_at + HEAD] = dot_nn(score_next[0:16], k_next).astype(jnp.bfloat16)
            for at, left_own, right_own, left_next, right_next in (
                (k_at, score_own, q_own, score_next, q_next),
                (v_at, prob_own, g_own, prob_next, g_next),
            ):
                near = dot_tn(left_own, right_own)
                far = dot_tn(left_next, right_next)
                split = FRAMES - HALO
                gq[0:split, at : at + HEAD] = near[HALO : HALO + split].astype(jnp.bfloat16)
                gq[split:FRAMES, at : at + HEAD] = (near[HALO + split : AHEAD] + far[0:HALO]).astype(jnp.bfloat16)
                gq[FRAMES:GROWS, at : at + HEAD] = far[HALO : HALO + 16].astype(jnp.bfloat16)
        for section in range(3):
            g_ref[:, pl.ds(pl.multiple_of(section * WIDTH + pair * PAIR, PAIR), PAIR)] = gq[
                0:FRAMES, section * PAIR : (section + 1) * PAIR
            ]
        gh[...] += dot_nt(gq[...], w)
        return 0

    lax.fori_loop(0, HEADS // 2, two_heads, 0)

    gc[...] = gh[...] * slope[HALO : HALO + GROWS, :]

    def spread_rows(step, _):
        row = pl.multiple_of(step * 16, 16)
        total = gh[pl.ds(row, 16), :]
        window = gc[pl.ds(row, 24), :]
        for tap in range(KERNEL):
            total = total + taps_ref[tap : tap + 1, :] * window[8 - tap : 24 - tap]
        gin_ref[0, pl.ds(row, 16), :] = jnp.where(live_rows(begin + row, 16), total, 0.0).astype(jnp.bfloat16)
        return 0

    lax.fori_loop(0, FRAMES // 16, spread_rows, 0)


def compute(where, x, xp, xn, c, cn, taps, w):
    vmem = pl.BlockSpec(memory_space=pltpu.VMEM)
    bf16, f32 = jnp.bfloat16, jnp.float32
    return pl.pallas_call(
        compute_kernel,
        out_shape=(
            jax.ShapeDtypeStruct((1, FRAMES, WIDTH), bf16),
            jax.ShapeDtypeStruct((1, FRAMES, WIDTH), bf16),
            jax.ShapeDtypeStruct((2, 2, WIDTH // 4, FRAMES), bf16),
            jax.ShapeDtypeStruct((FRAMES, 3 * WIDTH), bf16),
        ),
        in_specs=[pl.BlockSpec(memory_space=pltpu.SMEM)] + [vmem] * 6 + [pl.BlockSpec(memory_space=pl.ANY)],
        out_specs=(vmem,) * 4,
        scratch_shapes=[
            pltpu.VMEM((EXT + 8, WIDTH), f32),
            pltpu.VMEM((EXT, WIDTH), bf16),
            pltpu.VMEM((EXT, WIDTH), f32),
            pltpu.VMEM((AHEAD, WIDTH), bf16),
            pltpu.VMEM((FRAMES, AHEAD), f32),
            pltpu.VMEM((HALO, 2 * HALO), f32),
            pltpu.VMEM((EXT, SECTION), bf16),
            pltpu.VMEM((GROWS, SECTION), bf16),
            pltpu.VMEM((GROWS, WIDTH), f32),
            pltpu.VMEM((GROWS, WIDTH), f32),
            pltpu.VMEM((HEADS // 2, WIDTH, SECTION), bf16),
            pltpu.SemaphoreType.DMA((HEADS // 2, 3)),
        ],
        compiler_params=pltpu.CompilerParams(vmem_limit_bytes=40 * 1024 * 1024),
        name="compute",
    )(where, x, xp, xn, c, cn, taps, w)


def reduce_kernel(
    scale, ht_ref, g_ref, out_ref,
    hp, gp, wa, wb, r_ax, r_by, r_ay, r_bx, r_az, r_bz, send, recv,
):
    tm, dp = lax.axis_index("tm"), lax.axis_index("dp")
    core = lax.rem(tm, 2)
    zh = lax.rem(tm // 2, NZ // NZ_LO)
    x = tm // (2 * (NZ // NZ_LO))
    y = lax.rem(dp, NY)
    zl = dp // NY
    z = zh * NZ_LO + zl

    def device(x, y, z, core):
        return {
            "tm": (x * (NZ // NZ_LO) + z // NZ_LO) * 2 + core,
            "dp": lax.rem(z, NZ_LO) * NY + y,
        }

    partner = device(x, y, z, 1 - core)
    near = {
        ("x", 1): device(lax.rem(x + 1, NX), y, z, core),
        ("x", -1): device(lax.rem(x + NX - 1, NX), y, z, core),
        ("y", 1): device(x, lax.rem(y + 1, NY), z, core),
        ("y", -1): device(x, lax.rem(y + NY - 1, NY), z, core),
        ("z", 1): device(x, y, lax.rem(z + 1, NZ), core),
        ("z", -1): device(x, y, lax.rem(z + NZ - 1, NZ), core),
    }
    barrier = pltpu.get_barrier_semaphore()
    for other in [partner, *near.values()]:
        pl.semaphore_signal(barrier, inc=1, device_id=other, device_id_type=MESH)
    pl.semaphore_wait(barrier, 1 + len(near))

    slots = iter(range(64))
    copies = []

    def start(source, target, other):
        slot = next(slots)
        one = pltpu.make_async_remote_copy(
            src_ref=source,
            dst_ref=target,
            send_sem=send.at[slot],
            recv_sem=recv.at[slot],
            device_id=other,
            device_id_type=MESH,
        )
        one.start()
        copies.append(one)
        return one

    got_h = start(ht_ref.at[1 - core], hp, partner)
    got_g = start(g_ref, gp, partner)
    got_h.wait_recv()
    got_g.wait_recv()

    def products(part, store):
        left = jnp.concatenate([ht_ref[core, part], hp[part]], axis=1)

        def columns(step, _):
            at = pl.multiple_of(step * 256, 256)
            right = jnp.concatenate([g_ref[:, pl.ds(at, 256)], gp[:, pl.ds(at, 256)]], axis=0)
            product = dot_nn(left, right).astype(jnp.bfloat16)
            low, first = step // (NY // 2), lax.rem(step, NY // 2) * 2
            for row in range(NX):
                for high in range(NZ // NZ_LO):
                    for one in range(2):
                        group = row * (NZ // NZ_LO) + high
                        store(row, first + one, high * NZ_LO + low,
                              product[group * 16 : (group + 1) * 16, one * 128 : (one + 1) * 128])
            return 0

        lax.fori_loop(0, 12, columns, 0)

    def store_a(x, y, z, value):
        wa[x, y, z] = value

    def store_b(x, y, z, value):
        wb[y, x, z] = value

    class Stage:
        def __init__(self, axis, count, at, block, landing, halves):
            self.axis, self.count, self.at, self.block, self.landing = axis, count, at, block, landing
            far, less = count // 2, count // 2 - 1
            if halves:
                chains = [(1, 0, far), (-1, 1, far), (1, 1, less), (-1, 0, less)]
            else:
                chains = [(1, None, far), (-1, None, less)]
            self.chains, slot = [], 0
            for way, half, length in chains:
                self.chains.append((way, half, length, slot))
                slot += length
            self.pending = {}

        def place(self, way, distance):
            return lax.rem(self.at + self.count + way * distance, self.count)

        def step(self, number):
            for index, (way, half, length, slot) in enumerate(self.chains):
                lag = self.count // 2 - length
                s = number if lag == 0 else number - 0
                if s > length + 1:
                    continue
                ref = self.block(self.place(way, length - s + 1), half)
                if s > 1:
                    self.pending.pop(index).wait_recv()
                    landed = self.landing.at[slot + s - 2]
                    ref[...] = (ref[...].astype(jnp.float32) + landed[...].astype(jnp.float32)).astype(jnp.bfloat16)
                if s <= length:
                    self.pending[index] = start(ref, self.landing.at[slot + s - 1], near[self.axis, way])

    def half_of(ref, half, size):
        return ref if half is None else ref.at[pl.ds(half * (size // 2), size // 2)]

    a_x = Stage("x", NX, x, lambda at, half: half_of(wa.at[at], half, NY), r_ax, True)
    a_y = Stage("y", NY, y, lambda at, half: wa.at[x, at], r_ay, False)
    a_z = Stage("z", NZ, z, lambda at, half: wa.at[x, y, at], r_az, False)
    b_y = Stage("y", NY, y, lambda at, half: half_of(wb.at[at], half, NX), r_by, True)
    b_x = Stage("x", NX, x, lambda at, half: wb.at[y, at], r_bx, False)
    b_z = Stage("z", NZ, z, lambda at, half: wb.at[y, x, at], r_bz, False)

    products(1, store_b)
    b_y.step(1)
    products(0, store_a)
    a_x.step(1)
    b_y.step(2)
    a_x.step(2)
    b_y.step(3)
    b_y.step(4)
    a_x.step(3)
    a_y.step(1)
    b_y.step(5)
    b_x.step(1)
    a_y.step(2)
    b_x.step(2)
    a_y.step(3)
    b_x.step(3)
    b_z.step(1)
    a_y.step(4)
    b_z.step(2)
    a_y.step(5)
    a_z.step(1)
    for number in range(3, 7):
        b_z.step(number)
        a_z.step(number - 1)
    a_z_rest = (6,)
    for number in a_z_rest:
        a_z.step(number)

    def finish(part, stage, own):
        total = own.astype(jnp.float32)
        for index, (_, _, length, slot) in enumerate(stage.chains):
            if index in stage.pending:
                stage.pending.pop(index).wait_recv()
                total = total + stage.landing[slot + length - 1].astype(jnp.float32)
        out_ref[part * 16 : (part + 1) * 16, :] = total * scale

    finish(1, b_z, wb[y, x, z])
    finish(0, a_z, wa[x, y, z])
    for one in copies:
        one.wait_send()


def reduce_weight(ht, g, scale):
    vmem = pl.BlockSpec(memory_space=pltpu.VMEM)
    bf16 = jnp.bfloat16
    return pl.pallas_call(
        functools.partial(reduce_kernel, scale),
        out_shape=jax.ShapeDtypeStruct((32, HEAD), jnp.float32),
        in_specs=[vmem, vmem],
        out_specs=vmem,
        scratch_shapes=[
            pltpu.VMEM((2, WIDTH // 4, FRAMES), bf16),
            pltpu.VMEM((FRAMES, 3 * WIDTH), bf16),
            pltpu.VMEM((NX, NY, NZ, 16, HEAD), bf16),
            pltpu.VMEM((NY, NX, NZ, 16, HEAD), bf16),
            pltpu.VMEM((6, NY // 2, NZ, 16, HEAD), bf16),
            pltpu.VMEM((14, NX // 2, NZ, 16, HEAD), bf16),
            pltpu.VMEM((7, NZ, 16, HEAD), bf16),
            pltpu.VMEM((3, NZ, 16, HEAD), bf16),
            pltpu.VMEM((11, 16, HEAD), bf16),
            pltpu.VMEM((11, 16, HEAD), bf16),
            pltpu.SemaphoreType.DMA((64,)),
            pltpu.SemaphoreType.DMA((64,)),
        ],
        compiler_params=pltpu.CompilerParams(
            collective_id=1, has_side_effects=True, vmem_limit_bytes=40 * 1024 * 1024
        ),
        name="reduce",
    )(ht, g)


def on_device(frames_in, valid_frames, kernel, w_qkv, cotangent):
    frames = frames_in.shape[1]
    begin = lax.axis_index("tm") * frames
    where = jnp.concatenate([begin.astype(jnp.int32)[None], valid_frames])
    before, after, cot_after = exchange_halo(frames_in, cotangent)
    attended, grad_in, hidden_t, grad_qkv = compute(
        where, frames_in, before, after, cotangent, cot_after, kernel, w_qkv
    )
    scale = float(lax.axis_size("dp") * lax.axis_size("tm") * frames) ** (-0.5)
    block = reduce_weight(hidden_t, grad_qkv, scale)
    return (attended, grad_in, block.T[None])


def solution(mesh):
    return jax.shard_map(
        on_device,
        mesh=mesh,
        in_specs=(P("dp", "tm", None), P("dp"), P(), P(), P("dp", "tm", None)),
        out_specs=(P("dp", "tm", None), P("dp", "tm", None), P("dp", None, "tm")),
        check_vma=False,
    )
```

```python
import functools

import jax
import jax.numpy as jnp
from jax import lax
from jax.experimental import pallas as pl
from jax.experimental.pallas import tpu as pltpu
from jax.sharding import PartitionSpec as P

HEADS = 8
HEAD = 128
KERNEL = 9
LEFT = 70
HALO = 80
FRAMES = 128
WIDTH = 1024
EXT = HALO + FRAMES + HALO
AHEAD = FRAMES + HALO
GROWS = FRAMES + 16
PAIRS = HEADS // 2
PAIR = 2 * HEAD
SECTION = 3 * PAIR

NX, NY, NZ, NZ_LO = 4, 8, 12, 3
NZ_HI = NZ // NZ_LO
MESH = pl.DeviceIdType.MESH


def dot_nn(a, b):
    return lax.dot_general(a, b, (((1,), (0,)), ((), ())), preferred_element_type=jnp.float32)


def dot_nt(a, b):
    return lax.dot_general(a, b, (((1,), (1,)), ((), ())), preferred_element_type=jnp.float32)


def dot_tn(a, b):
    return lax.dot_general(a, b, (((0,), (0,)), ((), ())), preferred_element_type=jnp.float32)


def step_kernel(
    scale, count_ref, x_hbm, c_hbm, taps_ref, w_hbm,
    att_ref, gin_ref, out_ref,
    x_own, c_own, xp, xn, cn, ext, hid, slope, cot, mask_own, mask_next, wbuf, qkv, near, gq, gh, gc,
    ht_own, ht_prev, hr_own, hr_prev, g_own, g_prev, gr_own, gr_prev,
    wa, wb, r_ax, r_by, r_ay, r_bx, r_az, r_bz, local, send, recv,
):
    tm, dp = lax.axis_index("tm"), lax.axis_index("dp")
    steps = lax.axis_size("tm")
    core = lax.rem(tm, 2)
    zh = lax.rem(tm // 2, NZ_HI)
    x = tm // (2 * NZ_HI)
    y = lax.rem(dp, NY)
    zl = dp // NY
    z = zh * NZ_LO + zl
    begin = tm * FRAMES
    count = count_ref[0]
    factor = HEAD ** (-0.5)

    def device(x, y, z, core):
        return {"tm": (x * NZ_HI + z // NZ_LO) * 2 + core, "dp": lax.rem(z, NZ_LO) * NY + y}

    after, before = {"tm": lax.rem(tm + 1, steps)}, {"tm": lax.rem(tm + steps - 1, steps)}
    partner = device(x, y, z, 1 - core)
    near_by = {
        ("x", 1): device(lax.rem(x + 1, NX), y, z, core),
        ("x", -1): device(lax.rem(x + NX - 1, NX), y, z, core),
        ("y", 1): device(x, lax.rem(y + 1, NY), z, core),
        ("y", -1): device(x, lax.rem(y + NY - 1, NY), z, core),
    }
    column = [device(x, y, lax.rem(z + k, NZ), core) for k in range(1, NZ)]

    barrier = pltpu.get_barrier_semaphore()
    peers = [after, before, *near_by.values(), *column]
    for other in peers:
        pl.semaphore_signal(barrier, inc=1, device_id=other, device_id_type=MESH)

    order = [lax.rem(y // 2 + turn, PAIRS) for turn in (2, 1, 3, 0)]

    def weight(pair, section):
        return pltpu.make_async_copy(
            w_hbm.at[:, pl.ds(section * WIDTH + pair * PAIR, PAIR)],
            wbuf.at[pair, :, pl.ds(section * PAIR, PAIR)],
            local.at[2 + pair * 3 + section],
        )

    own = [
        pltpu.make_async_copy(x_hbm.at[0], x_own, local.at[0]),
        pltpu.make_async_copy(c_hbm.at[0], c_own, local.at[1]),
    ]
    for one in own:
        one.start()
    for pair in order:
        for section in range(3):
            weight(pair, section).start()

    pl.semaphore_wait(barrier, len(peers))

    slots = iter(range(SLOTS))
    sent = []

    def start(source, target, other):
        slot = next(slots)
        one = pltpu.make_async_remote_copy(
            src_ref=source,
            dst_ref=target,
            send_sem=send.at[slot],
            recv_sem=recv.at[slot],
            device_id=other,
            device_id_type=MESH,
        )
        one.start()
        sent.append(one)
        return one

    got_xp = start(x_hbm.at[0, pl.ds(FRAMES - HALO, HALO)], xp, after)
    got_xn = start(x_hbm.at[0, pl.ds(0, HALO)], xn, before)
    got_cn = start(c_hbm.at[0, pl.ds(0, HALO)], cn, before)

    def live_rows(first, rows):
        at = first + lax.broadcasted_iota(jnp.int32, (rows, 1), 0)
        return (at >= 0) & (at < count)

    def masked(first, value):
        return jnp.where(live_rows(first, value.shape[0]), value.astype(jnp.float32), 0.0)

    def band(rows, columns, first_query, first_key):
        query = first_query + lax.broadcasted_iota(jnp.int32, (rows, columns), 0)
        key = first_key + lax.broadcasted_iota(jnp.int32, (rows, columns), 1)
        offset = query - key
        allowed = (offset >= 0) & (offset <= LEFT) & (key >= 0) & (key < count) & (query < count)
        return jnp.where(allowed, 1.0, 0.0)

    def conv_rows(step, _):
        row = pl.multiple_of(step * 16, 16)
        window = ext[pl.ds(row, 24), :]
        total = jnp.zeros((16, WIDTH), jnp.float32)
        for tap in range(KERNEL):
            total = total + taps_ref[tap : tap + 1, :] * window[tap : tap + 16]
        logistic = 1.0 / (1.0 + jnp.exp(-total))
        hid[pl.ds(row, 16), :] = (window[8:24] + total * logistic).astype(jnp.bfloat16)
        slope[pl.ds(row, 16), :] = logistic * (1.0 + total * (1.0 - logistic))
        return 0

    def turn(first, take, target):
        for block in range(WIDTH // 128):
            tile = hid[first : first + FRAMES, block * 128 : (block + 1) * 128]
            turned = tile.astype(jnp.float32).T.astype(jnp.bfloat16)
            for piece in range(8):
                group = block * 2 + piece // 4
                rows = piece % 2 * (WIDTH // 4) + group * 16
                target[(piece // 2) % 2, rows : rows + 16, :] = turned[piece * 16 : (piece + 1) * 16, 0:take]

    inner = HALO + 16
    ext[0:8, :] = jnp.zeros((8, WIDTH), jnp.float32)
    mask_own[...] = band(FRAMES, AHEAD, begin, begin - HALO)
    mask_next[...] = band(HALO, 2 * HALO, begin + FRAMES, begin + FRAMES - HALO)
    own[0].wait()
    ext[8 + HALO : 8 + AHEAD, :] = masked(begin, x_own[...])
    lax.fori_loop(inner // 16, AHEAD // 16, conv_rows, 0)
    own[1].wait()
    cot[0:FRAMES, :] = masked(begin, c_own[...]).astype(jnp.bfloat16)
    for pair in order:
        for section in range(3):
            weight(pair, section).wait()
        qkv[pair, inner:AHEAD, :] = dot_nn(hid[inner:AHEAD, :], wbuf[pair]).astype(jnp.bfloat16)

    got_xp.wait_recv()
    ext[8 : 8 + HALO, :] = masked(begin - HALO, xp[...])
    lax.fori_loop(0, inner // 16, conv_rows, 0)
    turn(HALO, FRAMES, ht_own)
    turn(0, HALO, ht_prev)
    got_h = [start(ht_own.at[1 - core], hr_own, partner), start(ht_prev.at[1 - core], hr_prev, partner)]

    def attend(q, g, k, v, mask, first):
        raised = jnp.where(mask > 0.5, jnp.exp(dot_nt(q, k) * factor), 0.0)
        at = first + lax.broadcasted_iota(jnp.int32, (q.shape[0], 1), 0)
        missing = jnp.where(at < count, 0.0, 1.0)
        prob = raised * (1.0 / (jnp.sum(raised, axis=1, keepdims=True) + missing))
        grad_prob = dot_nt(g, v)
        mean = jnp.sum(prob * grad_prob, axis=1, keepdims=True)
        grad_score = (prob * (grad_prob - mean) * factor).astype(jnp.bfloat16)
        return prob.astype(jnp.bfloat16), grad_score

    def section_at(section, head):
        return slice(section * PAIR + head * HEAD, section * PAIR + (head + 1) * HEAD)

    def lanes(pair, head):
        return pl.ds(pl.multiple_of(pair * PAIR + head * HEAD, HEAD), HEAD)

    def attend_own(turn_no):
        pair = order[turn_no]
        qkv[pair, 0:inner, :] = dot_nn(hid[0:inner, :], wbuf[pair]).astype(jnp.bfloat16)
        for head in range(2):
            q = qkv[pair, HALO:AHEAD, section_at(0, head)]
            k = qkv[pair, 0:AHEAD, section_at(1, head)]
            v = qkv[pair, 0:AHEAD, section_at(2, head)]
            g = cot[0:FRAMES, lanes(pair, head)]
            prob, score = attend(q, g, k, v, mask_own[...], begin)
            att_ref[0, :, lanes(pair, head)] = dot_nn(prob, v).astype(jnp.bfloat16)
            g_own[turn_no, :, section_at(0, head)] = dot_nn(score, k).astype(jnp.bfloat16)
            for section, left, right in ((1, score, q), (2, prob, g)):
                total = dot_tn(left, right)
                g_prev[turn_no, :, section_at(section - 1, head)] = total[0:HALO].astype(jnp.bfloat16)
                g_own[turn_no, :, section_at(section, head)] = total[HALO:AHEAD].astype(jnp.bfloat16)
                near[turn_no, :, section_at(section - 1, head)] = total[HALO:AHEAD]
        return [
            start(g_own.at[turn_no], gr_own.at[turn_no], partner),
            start(g_prev.at[turn_no], gr_prev.at[turn_no], partner),
        ]

    def products(turn_no, landed):
        for one in landed:
            one.wait_recv()
        pair = order[turn_no]
        for section in range(3):
            at = slice(section * PAIR, (section + 1) * PAIR)
            if section == 0:
                left = jnp.concatenate([ht_own[core], hr_own[...]], axis=1)
                right = jnp.concatenate([g_own[turn_no, :, at], gr_own[turn_no, :, at]], axis=0)
                product = dot_nn(left, right)
            else:
                low = slice((section - 1) * PAIR, section * PAIR)
                product = dot_nn(
                    jnp.concatenate([ht_own[core], ht_prev[core]], axis=1),
                    jnp.concatenate([g_own[turn_no, :, at], g_prev[turn_no, :, low]], axis=0),
                ) + dot_nn(
                    jnp.concatenate([hr_own[...], hr_prev[...]], axis=1),
                    jnp.concatenate([gr_own[turn_no, :, at], gr_prev[turn_no, :, low]], axis=0),
                )
            product = product.astype(jnp.bfloat16)
            for part in range(2):
                for row in range(NX):
                    for high in range(NZ_HI):
                        first = ((part * NX + row) * NZ_HI + high) * 16
                        for head in range(2):
                            value = product[first : first + 16, head * HEAD : (head + 1) * HEAD]
                            if part == 0:
                                wa[row, pair * 2 + head, high * NZ_LO + section] = value
                            else:
                                wb[pair * 2 + head, row, high * NZ_LO + section] = value

    def add_into(ref, landed):
        total = ref[...].astype(jnp.float32)
        for one in landed:
            total = total + one[...].astype(jnp.float32)
        ref[...] = total.astype(jnp.bfloat16)

    class Chain:
        def __init__(self, axis, size, at, way, length, block, landing):
            self.to, self.size, self.at, self.way, self.length = near_by[axis, way], size, at, way, length
            self.block, self.landing, self.done, self.pending = block, landing, 0, None

        def step(self):
            self.done += 1
            place = lax.rem(self.at + self.size + self.way * (self.length - self.done + 1), self.size)
            ref = self.block(place)
            if self.pending is not None:
                self.pending.wait_recv()
                add_into(ref, [self.landing(self.done - 2)])
            self.pending = start(ref, self.landing(self.done - 1), self.to)

        def last(self):
            self.pending.wait_recv()
            return self.landing(self.length - 1)

    def half(ref, which, size):
        return ref.at[pl.ds(which * (size // 2), size // 2)]

    def four(axis, size, at, block, landing):
        far, less = size // 2, size // 2 - 1
        chains, slot = [], 0
        for way, which, length in ((1, 0, far), (-1, 1, far), (1, 1, less), (-1, 0, less)):
            chains.append(
                Chain(axis, size, at, way, length,
                      lambda place, which=which: block(place, which),
                      lambda step, slot=slot: landing.at[slot + step])
            )
            slot += length
        return chains

    def finish_four(chains, block, at):
        add_into(block(at, 0), [chains[0].last(), chains[3].last()])
        add_into(block(at, 1), [chains[1].last(), chains[2].last()])

    ax = []
    for turn_no in range(PAIRS):
        def head_block(place, which, turn_no=turn_no):
            return wa.at[place, order[turn_no] * 2 + which]
        ax.append((four("x", NX, x, head_block, r_ax.at[turn_no]), head_block))

    def by_block(place, which):
        return half(wb.at[place], which, NX)

    def ay_block(place, which):
        return half(wa.at[x, place], which, NZ)

    def bx_block(place, which):
        return half(wb.at[y, place], which, NZ)

    by = four("y", NY, y, by_block, r_by)
    ay = four("y", NY, y, ay_block, r_ay)
    bx = four("x", NX, x, bx_block, r_bx)

    def step_all(chains, which):
        for index in which:
            chains[index].step()

    def attend_next(turn_no):
        pair = order[turn_no]
        qkv[pair, AHEAD:EXT, :] = dot_nn(hid[AHEAD:EXT, :], wbuf[pair]).astype(jnp.bfloat16)
        gq[0:FRAMES, 0:PAIR] = g_own[turn_no, :, 0:PAIR]
        for head in range(2):
            q = qkv[pair, AHEAD:EXT, section_at(0, head)]
            k = qkv[pair, FRAMES:EXT, section_at(1, head)]
            v = qkv[pair, FRAMES:EXT, section_at(2, head)]
            g = cot[FRAMES:AHEAD, lanes(pair, head)]
            prob, score = attend(q, g, k, v, mask_next[...], begin + FRAMES)
            gq[FRAMES:GROWS, section_at(0, head)] = dot_nn(score[0:16], k).astype(jnp.bfloat16)
            split = FRAMES - HALO
            for section, left, right in ((1, score, q), (2, prob, g)):
                far = dot_tn(left, right)
                at = section_at(section, head)
                mine = near.at[turn_no, :, section_at(section - 1, head)]
                gq[0:split, at] = mine[0:split].astype(jnp.bfloat16)
                gq[split:FRAMES, at] = (mine[split:FRAMES] + far[0:HALO]).astype(jnp.bfloat16)
                gq[FRAMES:GROWS, at] = far[HALO : HALO + 16].astype(jnp.bfloat16)
        gh[...] += dot_nt(gq[...], wbuf[pair])

    def conv_next():
        got_xn.wait_recv()
        ext[8 + AHEAD : 8 + EXT, :] = masked(begin + FRAMES, xn[...])
        lax.fori_loop(AHEAD // 16, EXT // 16, conv_rows, 0)
        got_cn.wait_recv()
        cot[FRAMES:AHEAD, :] = masked(begin + FRAMES, cn[...]).astype(jnp.bfloat16)
        gh[...] = jnp.zeros_like(gh)

    def spread_rows(step, _):
        row = pl.multiple_of(step * 16, 16)
        total = gh[pl.ds(row, 16), :]
        window = gc[pl.ds(row, 24), :]
        for tap in range(KERNEL):
            total = total + taps_ref[tap : tap + 1, :] * window[8 - tap : 24 - tap]
        gin_ref[0, pl.ds(row, 16), :] = jnp.where(live_rows(begin + row, 16), total, 0.0).astype(jnp.bfloat16)
        return 0

    def spread():
        gc[...] = gh[...] * slope[HALO : HALO + GROWS, :]
        lax.fori_loop(0, FRAMES // 16, spread_rows, 0)

    def send_column(block, landing):
        return [
            start(block.at[lax.rem(z + k, NZ)], landing.at[k - 1], column[k - 1]) for k in range(1, NZ)
        ]

    def finish(part, own_block, landing, landed):
        total = own_block[z].astype(jnp.float32)
        for index, one in enumerate(landed):
            one.wait_recv()
            total = total + landing[index].astype(jnp.float32)
        out_ref[part * 16 : (part + 1) * 16, :] = total * scale

    sent_0 = attend_own(0)
    sent_1 = attend_own(1)
    for one in got_h:
        one.wait_recv()
    products(0, sent_0)
    step_all(ax[0][0], (0, 1, 2, 3))
    step_all(by, (0, 1))
    sent_2 = attend_own(2)
    products(1, sent_1)
    step_all(ax[1][0], (0, 1, 2, 3))
    step_all(by, (0, 2))
    step_all(ax[0][0], (0, 1))
    sent_3 = attend_own(3)
    products(2, sent_2)
    step_all(ax[2][0], (0, 1, 2, 3))
    step_all(by, (1, 3, 0, 2))
    step_all(ax[1][0], (0, 1))
    products(3, sent_3)
    step_all(ax[3][0], (0, 1, 2, 3))
    step_all(by, (1, 3, 0, 2))
    step_all(ax[2][0], (0, 1))
    conv_next()
    attend_next(0)
    step_all(ax[3][0], (0, 1))
    step_all(by, (1, 3))
    attend_next(1)
    attend_next(2)
    for chains, block in ax:
        finish_four(chains, block, x)
    step_all(ay, (0, 1, 2, 3))
    attend_next(3)
    finish_four(by, by_block, y)
    step_all(bx, (0, 1, 2, 3))
    step_all(ay, (0, 1, 2, 3))
    spread()
    step_all(bx, (0, 1))
    step_all(ay, (0, 1, 2, 3))
    finish_four(bx, bx_block, x)
    got_b = send_column(wb.at[y, x], r_bz)
    step_all(ay, (0, 1))
    finish_four(ay, ay_block, y)
    got_a = send_column(wa.at[x, y], r_az)
    finish(1, wb.at[y, x], r_bz, got_b)
    finish(0, wa.at[x, y], r_az, got_a)
    for one in sent:
        one.wait_send()


SLOTS = 112


def whole_step(frames_in, valid_frames, taps, w_qkv, cotangent):
    vmem, anywhere = pl.BlockSpec(memory_space=pltpu.VMEM), pl.BlockSpec(memory_space=pl.ANY)
    bf16, f32 = jnp.bfloat16, jnp.float32
    rows = jax.ShapeDtypeStruct((1, FRAMES, WIDTH), bf16)
    scale = float(lax.axis_size("dp") * lax.axis_size("tm") * FRAMES) ** (-0.5)
    scratch = [
        ((FRAMES, WIDTH), bf16), ((FRAMES, WIDTH), bf16),
        ((HALO, WIDTH), bf16), ((HALO, WIDTH), bf16), ((HALO, WIDTH), bf16),
        ((EXT + 8, WIDTH), f32), ((EXT, WIDTH), bf16), ((EXT, WIDTH), f32), ((AHEAD, WIDTH), bf16),
        ((FRAMES, AHEAD), f32), ((HALO, 2 * HALO), f32),
        ((PAIRS, WIDTH, SECTION), bf16), ((PAIRS, EXT, SECTION), bf16), ((PAIRS, FRAMES, 2 * PAIR), f32),
        ((GROWS, SECTION), bf16), ((GROWS, WIDTH), f32), ((GROWS, WIDTH), f32),
        ((2, WIDTH // 2, FRAMES), bf16), ((2, WIDTH // 2, HALO), bf16),
        ((WIDTH // 2, FRAMES), bf16), ((WIDTH // 2, HALO), bf16),
        ((PAIRS, FRAMES, SECTION), bf16), ((PAIRS, HALO, 2 * PAIR), bf16),
        ((PAIRS, FRAMES, SECTION), bf16), ((PAIRS, HALO, 2 * PAIR), bf16),
        ((NX, NY, NZ, 16, HEAD), bf16), ((NY, NX, NZ, 16, HEAD), bf16),
        ((PAIRS, 6, NZ, 16, HEAD), bf16), ((14, NX // 2, NZ, 16, HEAD), bf16),
        ((14, NZ // 2, 16, HEAD), bf16), ((6, NZ // 2, 16, HEAD), bf16),
        ((NZ - 1, 16, HEAD), bf16), ((NZ - 1, 16, HEAD), bf16),
    ]
    return pl.pallas_call(
        functools.partial(step_kernel, scale),
        out_shape=(rows, rows, jax.ShapeDtypeStruct((32, HEAD), f32)),
        in_specs=[pl.BlockSpec(memory_space=pltpu.SMEM), anywhere, anywhere, vmem, anywhere],
        out_specs=(vmem, vmem, vmem),
        scratch_shapes=[pltpu.VMEM(shape, kind) for shape, kind in scratch]
        + [pltpu.SemaphoreType.DMA((2 + 3 * PAIRS,)), pltpu.SemaphoreType.DMA((SLOTS,)), pltpu.SemaphoreType.DMA((SLOTS,))],
        compiler_params=pltpu.CompilerParams(
            collective_id=0, has_side_effects=True, vmem_limit_bytes=60 * 1024 * 1024
        ),
        name="step",
    )(valid_frames, frames_in, cotangent, taps, w_qkv)


def on_device(frames_in, valid_frames, kernel, w_qkv, cotangent):
    attended, grad_in, block = whole_step(frames_in, valid_frames, kernel, w_qkv, cotangent)
    return (attended, grad_in, block.T[None])


def solution(mesh):
    return jax.shard_map(
        on_device,
        mesh=mesh,
        in_specs=(P("dp", "tm", None), P("dp"), P(), P(), P("dp", "tm", None)),
        out_specs=(P("dp", "tm", None), P("dp", "tm", None), P("dp", None, "tm")),
        check_vma=False,
    )
```

```python
import functools

import jax
import jax.numpy as jnp
from jax import lax
from jax.experimental import pallas as pl
from jax.experimental.pallas import tpu as pltpu
from jax.sharding import PartitionSpec as P

HEADS = 8
HEAD = 128
KERNEL = 9
LEFT = 70
HALO = 80
FRAMES = 128
WIDTH = 1024
EXT = HALO + FRAMES + HALO
AHEAD = FRAMES + HALO
GROWS = FRAMES + 16
PAIRS = HEADS // 2
ROWS_A, ROWS_B = 24, 8
PAIR = 2 * HEAD
SECTION = 3 * PAIR

NX, NY, NZ, NZ_LO = 4, 8, 12, 3
NZ_HI = NZ // NZ_LO
MESH = pl.DeviceIdType.MESH


def dot_nn(a, b):
    return lax.dot_general(a, b, (((1,), (0,)), ((), ())), preferred_element_type=jnp.float32)


def dot_nt(a, b):
    return lax.dot_general(a, b, (((1,), (1,)), ((), ())), preferred_element_type=jnp.float32)


def dot_tn(a, b):
    return lax.dot_general(a, b, (((0,), (0,)), ((), ())), preferred_element_type=jnp.float32)


def step_kernel(
    scale, count_ref, x_hbm, c_hbm, taps_hbm, w_hbm,
    att_ref, gin_ref, out_ref,
    taps_ref, x_own, c_own, xp, xn, cn, ext, hid, slope, cot, mask_own, mask_next, wbuf, qkv, near, gq, gh, gc,
    ht_own, ht_prev, hr_own, hr_prev, g_own, g_prev, gr_own, gr_prev,
    wa, wb, r_ax, r_by, r_ay, r_bx, r_az, r_bz, local, send, recv,
):
    tm, dp = lax.axis_index("tm"), lax.axis_index("dp")
    steps = lax.axis_size("tm")
    core = lax.rem(tm, 2)
    zh = lax.rem(tm // 2, NZ_HI)
    x = tm // (2 * NZ_HI)
    y = lax.rem(dp, NY)
    zl = dp // NY
    z = zh * NZ_LO + zl
    begin = tm * FRAMES
    count = count_ref[0]
    factor = HEAD ** (-0.5)

    def device(x, y, z, core):
        return {"tm": (x * NZ_HI + z // NZ_LO) * 2 + core, "dp": lax.rem(z, NZ_LO) * NY + y}

    after, before = {"tm": lax.rem(tm + 1, steps)}, {"tm": lax.rem(tm + steps - 1, steps)}
    partner = device(x, y, z, 1 - core)
    near_by = {
        ("x", 1): device(lax.rem(x + 1, NX), y, z, core),
        ("x", -1): device(lax.rem(x + NX - 1, NX), y, z, core),
        ("y", 1): device(x, lax.rem(y + 1, NY), z, core),
        ("y", -1): device(x, lax.rem(y + NY - 1, NY), z, core),
    }
    column = [device(x, y, lax.rem(z + k, NZ), core) for k in range(1, NZ)]

    barrier = pltpu.get_barrier_semaphore()
    peers = [after, before, *near_by.values(), *column]
    for other in peers:
        pl.semaphore_signal(barrier, inc=1, device_id=other, device_id_type=MESH)

    order = [lax.rem(y // 2 + turn, PAIRS) for turn in (2, 1, 3, 0)]

    def weight(pair, section):
        return pltpu.make_async_copy(
            w_hbm.at[:, pl.ds(section * WIDTH + pair * PAIR, PAIR)],
            wbuf.at[pair, :, pl.ds(section * PAIR, PAIR)],
            local.at[3 + pair * 3 + section],
        )

    own = [
        pltpu.make_async_copy(x_hbm.at[0], x_own, local.at[0]),
        pltpu.make_async_copy(c_hbm.at[0], c_own, local.at[1]),
        pltpu.make_async_copy(taps_hbm, taps_ref, local.at[2]),
    ]
    for one in own:
        one.start()
    for pair in order:
        for section in range(3):
            weight(pair, section).start()

    pl.semaphore_wait(barrier, len(peers))

    slots = iter(range(SLOTS))
    sent = []

    def start(source, target, other):
        slot = next(slots)
        one = pltpu.make_async_remote_copy(
            src_ref=source,
            dst_ref=target,
            send_sem=send.at[slot],
            recv_sem=recv.at[slot],
            device_id=other,
            device_id_type=MESH,
        )
        one.start()
        sent.append(one)
        return one

    got_xp = start(x_hbm.at[0, pl.ds(FRAMES - HALO, HALO)], xp, after)
    got_xn = start(x_hbm.at[0, pl.ds(0, HALO)], xn, before)
    got_cn = start(c_hbm.at[0, pl.ds(0, HALO)], cn, before)

    def live_rows(first, rows):
        at = first + lax.broadcasted_iota(jnp.int32, (rows, 1), 0)
        return (at >= 0) & (at < count)

    def masked(first, value):
        return jnp.where(live_rows(first, value.shape[0]), value.astype(jnp.float32), 0.0)

    def band(rows, columns, first_query, first_key):
        query = first_query + lax.broadcasted_iota(jnp.int32, (rows, columns), 0)
        key = first_key + lax.broadcasted_iota(jnp.int32, (rows, columns), 1)
        offset = query - key
        allowed = (offset >= 0) & (offset <= LEFT) & (key >= 0) & (key < count) & (query < count)
        return jnp.where(allowed, 1.0, 0.0)

    def conv_rows(step, _):
        row = pl.multiple_of(step * 16, 16)
        window = ext[pl.ds(row, 24), :]
        total = jnp.zeros((16, WIDTH), jnp.float32)
        for tap in range(KERNEL):
            total = total + taps_ref[tap : tap + 1, :] * window[tap : tap + 16]
        logistic = 1.0 / (1.0 + jnp.exp(-total))
        hid[pl.ds(row, 16), :] = (window[8:24] + total * logistic).astype(jnp.bfloat16)
        slope[pl.ds(row, 16), :] = logistic * (1.0 + total * (1.0 - logistic))
        return 0

    def turn(first, take, target):
        for block in range(WIDTH // 128):
            tile = hid[first : first + FRAMES, block * 128 : (block + 1) * 128]
            turned = tile.astype(jnp.float32).T[:, 0:take]
            for group in range(4):
                place, side, row = block * 2 + group // 2, group % 2, group * 32
                at_a, at_b = place * ROWS_A, NX * NZ_HI * ROWS_A + place * ROWS_B
                target[side, at_a : at_a + ROWS_A, :] = turned[row : row + ROWS_A].astype(jnp.bfloat16)
                target[side, at_b : at_b + ROWS_B, :] = turned[row + ROWS_A : row + 32].astype(jnp.bfloat16)

    inner = HALO + 16
    ext[0:8, :] = jnp.zeros((8, WIDTH), jnp.float32)
    mask_own[...] = band(FRAMES, AHEAD, begin, begin - HALO)
    mask_next[...] = band(HALO, 2 * HALO, begin + FRAMES, begin + FRAMES - HALO)
    own[0].wait()
    own[2].wait()
    ext[8 + HALO : 8 + AHEAD, :] = masked(begin, x_own[...])
    lax.fori_loop(inner // 16, AHEAD // 16, conv_rows, 0)
    own[1].wait()
    cot[0:FRAMES, :] = masked(begin, c_own[...]).astype(jnp.bfloat16)
    for pair in order:
        for section in range(3):
            weight(pair, section).wait()
        qkv[pair, inner:AHEAD, :] = dot_nn(hid[inner:AHEAD, :], wbuf[pair]).astype(jnp.bfloat16)

    got_xp.wait_recv()
    ext[8 : 8 + HALO, :] = masked(begin - HALO, xp[...])
    lax.fori_loop(0, inner // 16, conv_rows, 0)
    turn(HALO, FRAMES, ht_own)
    turn(0, HALO, ht_prev)
    got_h = [start(ht_own.at[1 - core], hr_own, partner), start(ht_prev.at[1 - core], hr_prev, partner)]

    def attend(q, g, k, v, mask, first):
        raised = jnp.where(mask > 0.5, jnp.exp(dot_nt(q, k) * factor), 0.0)
        at = first + lax.broadcasted_iota(jnp.int32, (q.shape[0], 1), 0)
        missing = jnp.where(at < count, 0.0, 1.0)
        prob = raised * (1.0 / (jnp.sum(raised, axis=1, keepdims=True) + missing))
        grad_prob = dot_nt(g, v)
        mean = jnp.sum(prob * grad_prob, axis=1, keepdims=True)
        grad_score = (prob * (grad_prob - mean) * factor).astype(jnp.bfloat16)
        return prob.astype(jnp.bfloat16), grad_score

    def section_at(section, head):
        return slice(section * PAIR + head * HEAD, section * PAIR + (head + 1) * HEAD)

    def lanes(pair, head):
        return pl.ds(pl.multiple_of(pair * PAIR + head * HEAD, HEAD), HEAD)

    def attend_own(turn_no):
        pair = order[turn_no]
        qkv[pair, 0:inner, :] = dot_nn(hid[0:inner, :], wbuf[pair]).astype(jnp.bfloat16)
        for head in range(2):
            q = qkv[pair, HALO:AHEAD, section_at(0, head)]
            k = qkv[pair, 0:AHEAD, section_at(1, head)]
            v = qkv[pair, 0:AHEAD, section_at(2, head)]
            g = cot[0:FRAMES, lanes(pair, head)]
            prob, score = attend(q, g, k, v, mask_own[...], begin)
            att_ref[0, :, lanes(pair, head)] = dot_nn(prob, v).astype(jnp.bfloat16)
            g_own[turn_no, :, section_at(0, head)] = dot_nn(score, k).astype(jnp.bfloat16)
            for section, left, right in ((1, score, q), (2, prob, g)):
                total = dot_tn(left, right)
                g_prev[turn_no, :, section_at(section - 1, head)] = total[0:HALO].astype(jnp.bfloat16)
                g_own[turn_no, :, section_at(section, head)] = total[HALO:AHEAD].astype(jnp.bfloat16)
                near[turn_no, :, section_at(section - 1, head)] = total[HALO:AHEAD]
        return [
            start(g_own.at[turn_no], gr_own.at[turn_no], partner),
            start(g_prev.at[turn_no], gr_prev.at[turn_no], partner),
        ]

    def products(turn_no, landed):
        for one in landed:
            one.wait_recv()
        pair = order[turn_no]
        for section in range(3):
            at = slice(section * PAIR, (section + 1) * PAIR)
            if section == 0:
                left = jnp.concatenate([ht_own[core], hr_own[...]], axis=1)
                right = jnp.concatenate([g_own[turn_no, :, at], gr_own[turn_no, :, at]], axis=0)
                product = dot_nn(left, right)
            else:
                low = slice((section - 1) * PAIR, section * PAIR)
                product = dot_nn(
                    jnp.concatenate([ht_own[core], ht_prev[core]], axis=1),
                    jnp.concatenate([g_own[turn_no, :, at], g_prev[turn_no, :, low]], axis=0),
                ) + dot_nn(
                    jnp.concatenate([hr_own[...], hr_prev[...]], axis=1),
                    jnp.concatenate([gr_own[turn_no, :, at], gr_prev[turn_no, :, low]], axis=0),
                )
            for row in range(NX):
                for high in range(NZ_HI):
                    place = row * NZ_HI + high
                    at_a, at_b = place * ROWS_A, NX * NZ_HI * ROWS_A + place * ROWS_B
                    for head in range(2):
                        lane = slice(head * HEAD, (head + 1) * HEAD)
                        wa[row, pair * 2 + head, high * NZ_LO + section] = product[
                            at_a : at_a + ROWS_A, lane
                        ].astype(jnp.bfloat16)
                        wb[pair * 2 + head, row, high * NZ_LO + section] = product[
                            at_b : at_b + ROWS_B, lane
                        ].astype(jnp.bfloat16)

    def add_into(ref, landed):
        total = ref[...].astype(jnp.float32)
        for one in landed:
            total = total + one[...].astype(jnp.float32)
        ref[...] = total.astype(jnp.bfloat16)

    class Chain:
        def __init__(self, axis, size, at, way, length, block, landing):
            self.to, self.size, self.at, self.way, self.length = near_by[axis, way], size, at, way, length
            self.block, self.landing, self.done, self.pending = block, landing, 0, None

        def step(self):
            self.done += 1
            place = lax.rem(self.at + self.size + self.way * (self.length - self.done + 1), self.size)
            ref = self.block(place)
            if self.pending is not None:
                self.pending.wait_recv()
                add_into(ref, [self.landing(self.done - 2)])
            self.pending = start(ref, self.landing(self.done - 1), self.to)

        def last(self):
            self.pending.wait_recv()
            return self.landing(self.length - 1)

    def half(ref, which, size):
        return ref.at[pl.ds(which * (size // 2), size // 2)]

    def four(axis, size, at, block, landing):
        far, less = size // 2, size // 2 - 1
        chains, slot = [], 0
        for way, which, length in ((1, 0, far), (-1, 1, far), (1, 1, less), (-1, 0, less)):
            chains.append(
                Chain(axis, size, at, way, length,
                      lambda place, which=which: block(place, which),
                      lambda step, slot=slot: landing.at[slot + step])
            )
            slot += length
        return chains

    def finish_four(chains, block, at):
        add_into(block(at, 0), [chains[0].last(), chains[3].last()])
        add_into(block(at, 1), [chains[1].last(), chains[2].last()])

    ax = []
    for turn_no in range(PAIRS):
        def head_block(place, which, turn_no=turn_no):
            return wa.at[place, order[turn_no] * 2 + which]
        ax.append((four("x", NX, x, head_block, r_ax.at[turn_no]), head_block))

    def by_block(place, which):
        return half(wb.at[place], which, NX)

    def ay_block(place, which):
        return half(wa.at[x, place], which, NZ)

    def bx_block(place, which):
        return half(wb.at[y, place], which, NZ)

    by = four("y", NY, y, by_block, r_by)
    ay = four("y", NY, y, ay_block, r_ay)
    bx = four("x", NX, x, bx_block, r_bx)

    def step_all(chains, which):
        for index in which:
            chains[index].step()

    def attend_next(turn_no):
        pair = order[turn_no]
        qkv[pair, AHEAD:EXT, :] = dot_nn(hid[AHEAD:EXT, :], wbuf[pair]).astype(jnp.bfloat16)
        gq[0:FRAMES, 0:PAIR] = g_own[turn_no, :, 0:PAIR]
        for head in range(2):
            q = qkv[pair, AHEAD:EXT, section_at(0, head)]
            k = qkv[pair, FRAMES:EXT, section_at(1, head)]
            v = qkv[pair, FRAMES:EXT, section_at(2, head)]
            g = cot[FRAMES:AHEAD, lanes(pair, head)]
            prob, score = attend(q, g, k, v, mask_next[...], begin + FRAMES)
            gq[FRAMES:GROWS, section_at(0, head)] = dot_nn(score[0:16], k).astype(jnp.bfloat16)
            split = FRAMES - HALO
            for section, left, right in ((1, score, q), (2, prob, g)):
                far = dot_tn(left, right)
                at = section_at(section, head)
                mine = near.at[turn_no, :, section_at(section - 1, head)]
                gq[0:split, at] = mine[0:split].astype(jnp.bfloat16)
                gq[split:FRAMES, at] = (mine[split:FRAMES] + far[0:HALO]).astype(jnp.bfloat16)
                gq[FRAMES:GROWS, at] = far[HALO : HALO + 16].astype(jnp.bfloat16)
        gh[...] += dot_nt(gq[...], wbuf[pair])

    def conv_next():
        got_xn.wait_recv()
        ext[8 + AHEAD : 8 + EXT, :] = masked(begin + FRAMES, xn[...])
        lax.fori_loop(AHEAD // 16, EXT // 16, conv_rows, 0)
        got_cn.wait_recv()
        cot[FRAMES:AHEAD, :] = masked(begin + FRAMES, cn[...]).astype(jnp.bfloat16)
        gh[...] = jnp.zeros_like(gh)

    def spread_rows(step, _):
        row = pl.multiple_of(step * 16, 16)
        total = gh[pl.ds(row, 16), :]
        window = gc[pl.ds(row, 24), :]
        for tap in range(KERNEL):
            total = total + taps_ref[tap : tap + 1, :] * window[8 - tap : 24 - tap]
        gin_ref[0, pl.ds(row, 16), :] = jnp.where(live_rows(begin + row, 16), total, 0.0).astype(jnp.bfloat16)
        return 0

    def spread():
        gc[...] = gh[...] * slope[HALO : HALO + GROWS, :]
        lax.fori_loop(0, FRAMES // 16, spread_rows, 0)

    def send_column(block, landing):
        return [
            start(block.at[lax.rem(z + k, NZ)], landing.at[k - 1], column[k - 1]) for k in range(1, NZ)
        ]

    def finish(rows, own_block, landing, landed):
        total = own_block[z].astype(jnp.float32)
        for index, one in enumerate(landed):
            one.wait_recv()
            total = total + landing[index].astype(jnp.float32)
        out_ref[rows, :] = total * scale

    def finish_ax(turn_no):
        chains, block = ax[turn_no]
        finish_four(chains, block, x)

    sent_0 = attend_own(0)
    sent_1 = attend_own(1)
    for one in got_h:
        one.wait_recv()
    products(0, sent_0)
    step_all(ax[0][0], (0, 1, 2, 3))
    step_all(by, (0, 1))
    sent_2 = attend_own(2)
    products(1, sent_1)
    step_all(ax[1][0], (0, 1, 2, 3))
    step_all(by, (0, 2))
    step_all(ax[0][0], (0, 1))
    sent_3 = attend_own(3)
    products(2, sent_2)
    step_all(ax[2][0], (0, 1, 2, 3))
    step_all(by, (1, 3, 0, 2))
    products(3, sent_3)
    step_all(ax[1][0], (0, 1))
    step_all(ax[3][0], (0, 1, 2, 3))
    step_all(by, (1, 3, 0, 2))
    conv_next()
    step_all(ax[2][0], (0, 1))
    step_all(by, (1, 3))
    attend_next(0)
    finish_ax(0)
    step_all(ay, (0, 1))
    step_all(ax[3][0], (0, 1))
    attend_next(1)
    finish_four(by, by_block, y)
    step_all(bx, (0, 1, 2, 3))
    finish_ax(1)
    step_all(ay, (0, 2))
    attend_next(2)
    step_all(ay, (0, 2))
    step_all(bx, (0, 1))
    finish_ax(2)
    step_all(ay, (1, 3))
    attend_next(3)
    step_all(ay, (1, 3))
    finish_four(bx, bx_block, x)
    got_b = send_column(wb.at[y, x], r_bz)
    finish_ax(3)
    step_all(ay, (0, 1, 2, 3))
    spread()
    finish_four(ay, ay_block, y)
    got_a = send_column(wa.at[x, y], r_az)
    finish(slice(ROWS_A, ROWS_A + ROWS_B), wb.at[y, x], r_bz, got_b)
    finish(slice(0, ROWS_A), wa.at[x, y], r_az, got_a)
    for one in sent:
        one.wait_send()


SLOTS = 112


def whole_step(frames_in, valid_frames, taps, w_qkv, cotangent):
    vmem, anywhere = pl.BlockSpec(memory_space=pltpu.VMEM), pl.BlockSpec(memory_space=pl.ANY)
    bf16, f32 = jnp.bfloat16, jnp.float32
    rows = jax.ShapeDtypeStruct((1, FRAMES, WIDTH), bf16)
    scale = float(lax.axis_size("dp") * lax.axis_size("tm") * FRAMES) ** (-0.5)
    scratch = [
        ((KERNEL, WIDTH), f32), ((FRAMES, WIDTH), bf16), ((FRAMES, WIDTH), bf16),
        ((HALO, WIDTH), bf16), ((HALO, WIDTH), bf16), ((HALO, WIDTH), bf16),
        ((EXT + 8, WIDTH), f32), ((EXT, WIDTH), bf16), ((EXT, WIDTH), f32), ((AHEAD, WIDTH), bf16),
        ((FRAMES, AHEAD), f32), ((HALO, 2 * HALO), f32),
        ((PAIRS, WIDTH, SECTION), bf16), ((PAIRS, EXT, SECTION), bf16), ((PAIRS, FRAMES, 2 * PAIR), f32),
        ((GROWS, SECTION), bf16), ((GROWS, WIDTH), f32), ((GROWS, WIDTH), f32),
        ((2, WIDTH // 2, FRAMES), bf16), ((2, WIDTH // 2, HALO), bf16),
        ((WIDTH // 2, FRAMES), bf16), ((WIDTH // 2, HALO), bf16),
        ((PAIRS, FRAMES, SECTION), bf16), ((PAIRS, HALO, 2 * PAIR), bf16),
        ((PAIRS, FRAMES, SECTION), bf16), ((PAIRS, HALO, 2 * PAIR), bf16),
        ((NX, NY, NZ, ROWS_A, HEAD), bf16), ((NY, NX, NZ, ROWS_B, HEAD), bf16),
        ((PAIRS, 6, NZ, ROWS_A, HEAD), bf16), ((14, NX // 2, NZ, ROWS_B, HEAD), bf16),
        ((14, NZ // 2, ROWS_A, HEAD), bf16), ((6, NZ // 2, ROWS_B, HEAD), bf16),
        ((NZ - 1, ROWS_A, HEAD), bf16), ((NZ - 1, ROWS_B, HEAD), bf16),
    ]
    return pl.pallas_call(
        functools.partial(step_kernel, scale),
        out_shape=(rows, rows, jax.ShapeDtypeStruct((32, HEAD), f32)),
        in_specs=[pl.BlockSpec(memory_space=pltpu.SMEM)] + [anywhere] * 4,
        out_specs=(vmem, vmem, vmem),
        scratch_shapes=[pltpu.VMEM(shape, kind) for shape, kind in scratch]
        + [pltpu.SemaphoreType.DMA((3 + 3 * PAIRS,)), pltpu.SemaphoreType.DMA((SLOTS,)), pltpu.SemaphoreType.DMA((SLOTS,))],
        compiler_params=pltpu.CompilerParams(
            collective_id=0, has_side_effects=True, vmem_limit_bytes=54500 * 1024
        ),
        name="step",
    )(valid_frames, frames_in, cotangent, taps, w_qkv)


def on_device(frames_in, valid_frames, kernel, w_qkv, cotangent):
    attended, grad_in, block = whole_step(frames_in, valid_frames, kernel, w_qkv, cotangent)
    return (attended, grad_in, block.T[None])


def solution(mesh):
    return jax.shard_map(
        on_device,
        mesh=mesh,
        in_specs=(P("dp", "tm", None), P("dp"), P(), P(), P("dp", "tm", None)),
        out_specs=(P("dp", "tm", None), P("dp", "tm", None), P("dp", None, "tm")),
        check_vma=False,
    )
```

```python
import functools

import jax
import jax.numpy as jnp
from jax import lax
from jax.experimental import pallas as pl
from jax.experimental.pallas import tpu as pltpu
from jax.sharding import PartitionSpec as P

HEADS = 8
HEAD = 128
KERNEL = 9
LEFT = 70
HALO = 80
FRAMES = 128
WIDTH = 1024
EXT = HALO + FRAMES + HALO
AHEAD = FRAMES + HALO
GROWS = FRAMES + 16
PAIRS = HEADS // 2
ROWS_A, ROWS_B = 64, 32
PAIR = 2 * HEAD
SECTION = 3 * PAIR

NX, NY, NZ, NZ_LO = 4, 8, 12, 3
NZ_HI = NZ // NZ_LO
MESH = pl.DeviceIdType.MESH


def dot_nn(a, b):
    return lax.dot_general(a, b, (((1,), (0,)), ((), ())), preferred_element_type=jnp.float32)


def dot_nt(a, b):
    return lax.dot_general(a, b, (((1,), (1,)), ((), ())), preferred_element_type=jnp.float32)


def dot_tn(a, b):
    return lax.dot_general(a, b, (((0,), (0,)), ((), ())), preferred_element_type=jnp.float32)


def step_kernel(
    scale, count_ref, x_hbm, c_hbm, taps_hbm, w_hbm,
    att_ref, gin_ref, out_ref,
    taps_ref, x_own, c_own, xp, xn, cn, ext, hid, slope, cot, mask_own, mask_next, wbuf, qkv, near, gq, gh, gc,
    ht_own, ht_prev, hr_own, hr_prev, g_own, g_prev, gr_own, gr_prev,
    wa, wb, r_ax, r_by, r_ay, r_bx, last, r_z, local, send, recv,
):
    tm, dp = lax.axis_index("tm"), lax.axis_index("dp")
    steps = lax.axis_size("tm")
    core = lax.rem(tm, 2)
    zh = lax.rem(tm // 2, NZ_HI)
    x = tm // (2 * NZ_HI)
    y = lax.rem(dp, NY)
    zl = dp // NY
    z = zh * NZ_LO + zl
    begin = tm * FRAMES
    count = count_ref[0]
    factor = HEAD ** (-0.5)

    def device(x, y, z, core):
        return {"tm": (x * NZ_HI + z // NZ_LO) * 2 + core, "dp": lax.rem(z, NZ_LO) * NY + y}

    after, before = {"tm": lax.rem(tm + 1, steps)}, {"tm": lax.rem(tm + steps - 1, steps)}
    partner = device(x, y, z, 1 - core)
    near_by = {
        ("x", 1): device(lax.rem(x + 1, NX), y, z, core),
        ("x", -1): device(lax.rem(x + NX - 1, NX), y, z, core),
        ("y", 1): device(x, lax.rem(y + 1, NY), z, core),
        ("y", -1): device(x, lax.rem(y + NY - 1, NY), z, core),
    }
    column = [device(x, y, lax.rem(z + k, NZ), core) for k in range(1, NZ)]

    barrier = pltpu.get_barrier_semaphore()
    peers = [after, before, *near_by.values(), *column]
    for other in peers:
        pl.semaphore_signal(barrier, inc=1, device_id=other, device_id_type=MESH)

    order = [lax.rem(y // 2 + turn, PAIRS) for turn in (2, 1, 3, 0)]

    def weight(pair, section):
        return pltpu.make_async_copy(
            w_hbm.at[:, pl.ds(section * WIDTH + pair * PAIR, PAIR)],
            wbuf.at[pair, :, pl.ds(section * PAIR, PAIR)],
            local.at[3 + pair * 3 + section],
        )

    pl.semaphore_wait(barrier, len(peers))

    slots = iter(range(SLOTS))
    sent = []

    def start(source, target, other):
        slot = next(slots)
        one = pltpu.make_async_remote_copy(
            src_ref=source,
            dst_ref=target,
            send_sem=send.at[slot],
            recv_sem=recv.at[slot],
            device_id=other,
            device_id_type=MESH,
        )
        one.start()
        sent.append(one)
        return one

    got_xp = start(x_hbm.at[0, pl.ds(FRAMES - HALO, HALO)], xp, after)
    got_xn = start(x_hbm.at[0, pl.ds(0, HALO)], xn, before)
    own = [
        pltpu.make_async_copy(x_hbm.at[0], x_own, local.at[0]),
        pltpu.make_async_copy(taps_hbm, taps_ref, local.at[2]),
        pltpu.make_async_copy(c_hbm.at[0], c_own, local.at[1]),
    ]
    for one in own:
        one.start()
    got_cn = start(c_hbm.at[0, pl.ds(0, HALO)], cn, before)
    for pair in order:
        for section in range(3):
            weight(pair, section).start()

    def live_rows(first, rows):
        at = first + lax.broadcasted_iota(jnp.int32, (rows, 1), 0)
        return (at >= 0) & (at < count)

    def masked(first, value):
        return jnp.where(live_rows(first, value.shape[0]), value.astype(jnp.float32), 0.0)

    def band(rows, columns, first_query, first_key):
        query = first_query + lax.broadcasted_iota(jnp.int32, (rows, columns), 0)
        key = first_key + lax.broadcasted_iota(jnp.int32, (rows, columns), 1)
        offset = query - key
        allowed = (offset >= 0) & (offset <= LEFT) & (key >= 0) & (key < count) & (query < count)
        return jnp.where(allowed, 1.0, 0.0)

    def conv_rows(step, _):
        row = pl.multiple_of(step * 16, 16)
        window = ext[pl.ds(row, 24), :]
        total = jnp.zeros((16, WIDTH), jnp.float32)
        for tap in range(KERNEL):
            total = total + taps_ref[tap : tap + 1, :] * window[tap : tap + 16]
        logistic = 1.0 / (1.0 + jnp.exp(-total))
        hid[pl.ds(row, 16), :] = (window[8:24] + total * logistic).astype(jnp.bfloat16)
        slope[pl.ds(row, 16), :] = logistic * (1.0 + total * (1.0 - logistic))
        return 0

    def turn(first, take, target):
        for block in range(WIDTH // 128):
            tile = hid[first : first + FRAMES, block * 128 : (block + 1) * 128]
            turned = tile.astype(jnp.float32).T.astype(jnp.bfloat16)[:, 0:take]
            for group in range(4):
                place, side = (block * 2 + group // 2) * 32, group % 2
                target[side, place : place + 32, :] = turned[group * 32 : (group + 1) * 32]

    inner = HALO + 16
    ext[0:8, :] = jnp.zeros((8, WIDTH), jnp.float32)
    mask_own[...] = band(FRAMES, AHEAD, begin, begin - HALO)
    mask_next[...] = band(HALO, 2 * HALO, begin + FRAMES, begin + FRAMES - HALO)
    own[0].wait()
    own[1].wait()
    ext[8 + HALO : 8 + AHEAD, :] = masked(begin, x_own[...])
    lax.fori_loop(inner // 16, AHEAD // 16, conv_rows, 0)
    own[2].wait()
    cot[0:FRAMES, :] = masked(begin, c_own[...]).astype(jnp.bfloat16)
    for pair in order:
        for section in range(3):
            weight(pair, section).wait()
        qkv[pair, inner:AHEAD, :] = dot_nn(hid[inner:AHEAD, :], wbuf[pair]).astype(jnp.bfloat16)

    got_xp.wait_recv()
    ext[8 : 8 + HALO, :] = masked(begin - HALO, xp[...])
    lax.fori_loop(0, inner // 16, conv_rows, 0)
    turn(HALO, FRAMES, ht_own)
    turn(0, HALO, ht_prev)
    got_h = [start(ht_own.at[1 - core], hr_own, partner), start(ht_prev.at[1 - core], hr_prev, partner)]

    def attend(q, g, k, v, mask, first):
        raised = jnp.where(mask > 0.5, jnp.exp(dot_nt(q, k) * factor), 0.0)
        at = first + lax.broadcasted_iota(jnp.int32, (q.shape[0], 1), 0)
        missing = jnp.where(at < count, 0.0, 1.0)
        prob = raised * (1.0 / (jnp.sum(raised, axis=1, keepdims=True) + missing))
        grad_prob = dot_nt(g, v)
        mean = jnp.sum(prob * grad_prob, axis=1, keepdims=True)
        grad_score = (prob * (grad_prob - mean) * factor).astype(jnp.bfloat16)
        return prob.astype(jnp.bfloat16), grad_score

    def section_at(section, head):
        return slice(section * PAIR + head * HEAD, section * PAIR + (head + 1) * HEAD)

    def lanes(pair, head):
        return pl.ds(pl.multiple_of(pair * PAIR + head * HEAD, HEAD), HEAD)

    def attend_own(turn_no):
        pair = order[turn_no]
        qkv[pair, 0:inner, :] = dot_nn(hid[0:inner, :], wbuf[pair]).astype(jnp.bfloat16)
        for head in range(2):
            q = qkv[pair, HALO:AHEAD, section_at(0, head)]
            k = qkv[pair, 0:AHEAD, section_at(1, head)]
            v = qkv[pair, 0:AHEAD, section_at(2, head)]
            g = cot[0:FRAMES, lanes(pair, head)]
            prob, score = attend(q, g, k, v, mask_own[...], begin)
            att_ref[0, :, lanes(pair, head)] = dot_nn(prob, v).astype(jnp.bfloat16)
            g_own[turn_no, :, section_at(0, head)] = dot_nn(score, k).astype(jnp.bfloat16)
            for section, left, right in ((1, score, q), (2, prob, g)):
                total = dot_tn(left, right)
                g_prev[turn_no, :, section_at(section - 1, head)] = total[0:HALO].astype(jnp.bfloat16)
                g_own[turn_no, :, section_at(section, head)] = total[HALO:AHEAD].astype(jnp.bfloat16)
                near[turn_no, :, section_at(section - 1, head)] = total[HALO:AHEAD]
        return [
            start(g_own.at[turn_no], gr_own.at[turn_no], partner),
            start(g_prev.at[turn_no], gr_prev.at[turn_no], partner),
        ]

    def products(turn_no, landed):
        for one in landed:
            one.wait_recv()
        pair = order[turn_no]
        for section in range(3):
            at = slice(section * PAIR, (section + 1) * PAIR)
            if section == 0:
                left = jnp.concatenate([ht_own[core], hr_own[...]], axis=1)
                right = jnp.concatenate([g_own[turn_no, :, at], gr_own[turn_no, :, at]], axis=0)
                product = dot_nn(left, right)
            else:
                low = slice((section - 1) * PAIR, section * PAIR)
                product = dot_nn(
                    jnp.concatenate([ht_own[core], ht_prev[core]], axis=1),
                    jnp.concatenate([g_own[turn_no, :, at], g_prev[turn_no, :, low]], axis=0),
                ) + dot_nn(
                    jnp.concatenate([hr_own[...], hr_prev[...]], axis=1),
                    jnp.concatenate([gr_own[turn_no, :, at], gr_prev[turn_no, :, low]], axis=0),
                )
            product = product.astype(jnp.bfloat16)
            for row in range(NX):
                for high in range(NZ_HI):
                    first = (row * NZ_HI + high) * 32
                    for head in range(2):
                        value = product[first : first + 32, head * HEAD : (head + 1) * HEAD]
                        if section == 0:
                            wa[row, pair * 2 + head, high, 0:32, :] = value
                        else:
                            at_a, at_b = 16 + section * 16, section * 16 - 16
                            wa[row, pair * 2 + head, high, at_a : at_a + 16, :] = value[0:16]
                            wb[pair * 2 + head, row, high, at_b : at_b + 16, :] = value[16:32]

    def add_into(ref, landed):
        total = ref[...].astype(jnp.float32)
        for one in landed:
            total = total + one[...].astype(jnp.float32)
        ref[...] = total.astype(jnp.bfloat16)

    class Chain:
        def __init__(self, axis, size, at, way, length, block, landing):
            self.to, self.size, self.at, self.way, self.length = near_by[axis, way], size, at, way, length
            self.block, self.landing, self.done, self.pending = block, landing, 0, None

        def step(self):
            self.done += 1
            place = lax.rem(self.at + self.size + self.way * (self.length - self.done + 1), self.size)
            ref = self.block(place)
            if self.pending is not None:
                self.pending.wait_recv()
                add_into(ref, [self.landing(self.done - 2)])
            self.pending = start(ref, self.landing(self.done - 1), self.to)

        def last(self):
            self.pending.wait_recv()
            return self.landing(self.length - 1)

    def half(ref, which, size):
        return ref.at[pl.ds(which * (size // 2), size // 2)]

    def four(axis, size, at, block, landing):
        far, less = size // 2, size // 2 - 1
        chains, slot = [], 0
        for way, which, length in ((1, 0, far), (-1, 1, far), (1, 1, less), (-1, 0, less)):
            chains.append(
                Chain(axis, size, at, way, length,
                      lambda place, which=which: block(place, which),
                      lambda step, slot=slot: landing.at[slot + step])
            )
            slot += length
        return chains

    def finish_four(chains, block, at):
        add_into(block(at, 0), [chains[0].last(), chains[3].last()])
        add_into(block(at, 1), [chains[1].last(), chains[2].last()])

    ax = []
    for turn_no in range(PAIRS):
        def head_block(place, which, turn_no=turn_no):
            return wa.at[place, order[turn_no] * 2 + which]
        ax.append((four("x", NX, x, head_block, r_ax.at[turn_no]), head_block))

    def by_block(place, which):
        return half(wb.at[place], which, NX)

    def ay_block(place, which):
        return half(wa.at[x, place], which, NZ_HI)

    def bx_block(place, which):
        return half(wb.at[y, place], which, NZ_HI)

    by = four("y", NY, y, by_block, r_by)
    ay = four("y", NY, y, ay_block, r_ay)
    bx = four("x", NX, x, bx_block, r_bx)

    def step_all(chains, which):
        for index in which:
            chains[index].step()

    def attend_next(turn_no):
        pair = order[turn_no]
        qkv[pair, AHEAD:EXT, :] = dot_nn(hid[AHEAD:EXT, :], wbuf[pair]).astype(jnp.bfloat16)
        gq[0:FRAMES, 0:PAIR] = g_own[turn_no, :, 0:PAIR]
        for head in range(2):
            q = qkv[pair, AHEAD:EXT, section_at(0, head)]
            k = qkv[pair, FRAMES:EXT, section_at(1, head)]
            v = qkv[pair, FRAMES:EXT, section_at(2, head)]
            g = cot[FRAMES:AHEAD, lanes(pair, head)]
            prob, score = attend(q, g, k, v, mask_next[...], begin + FRAMES)
            gq[FRAMES:GROWS, section_at(0, head)] = dot_nn(score[0:16], k).astype(jnp.bfloat16)
            split = FRAMES - HALO
            for section, left, right in ((1, score, q), (2, prob, g)):
                far = dot_tn(left, right)
                at = section_at(section, head)
                mine = near.at[turn_no, :, section_at(section - 1, head)]
                gq[0:split, at] = mine[0:split].astype(jnp.bfloat16)
                gq[split:FRAMES, at] = (mine[split:FRAMES] + far[0:HALO]).astype(jnp.bfloat16)
                gq[FRAMES:GROWS, at] = far[HALO : HALO + 16].astype(jnp.bfloat16)
        gh[...] += dot_nt(gq[...], wbuf[pair])

    def conv_next():
        got_xn.wait_recv()
        ext[8 + AHEAD : 8 + EXT, :] = masked(begin + FRAMES, xn[...])
        lax.fori_loop(AHEAD // 16, EXT // 16, conv_rows, 0)
        got_cn.wait_recv()
        cot[FRAMES:AHEAD, :] = masked(begin + FRAMES, cn[...]).astype(jnp.bfloat16)
        gh[...] = jnp.zeros_like(gh)

    def spread_rows(step, _):
        row = pl.multiple_of(step * 16, 16)
        total = gh[pl.ds(row, 16), :]
        window = gc[pl.ds(row, 24), :]
        for tap in range(KERNEL):
            total = total + taps_ref[tap : tap + 1, :] * window[8 - tap : 24 - tap]
        gin_ref[0, pl.ds(row, 16), :] = jnp.where(live_rows(begin + row, 16), total, 0.0).astype(jnp.bfloat16)
        return 0

    def spread():
        gc[...] = gh[...] * slope[HALO : HALO + GROWS, :]
        lax.fori_loop(0, FRAMES // 16, spread_rows, 0)

    def send_column():
        for high in range(NZ_HI):
            last[high * NZ_LO] = wa[x, y, high, 0:32, :]
            for section in range(1, NZ_LO):
                at_a, at_b = 16 + section * 16, section * 16 - 16
                last[high * NZ_LO + section, 0:16, :] = wa[x, y, high, at_a : at_a + 16, :]
                last[high * NZ_LO + section, 16:32, :] = wb[y, x, high, at_b : at_b + 16, :]
        far_first = sorted(range(1, NZ), key=lambda k: abs(k - NZ // 2))
        return {k: start(last.at[lax.rem(z + k, NZ)], r_z.at[k - 1], column[k - 1]) for k in far_first}

    def finish(landed):
        total = last[z].astype(jnp.float32)
        for k in sorted(landed, key=lambda k: -abs(k - NZ // 2)):
            landed[k].wait_recv()
            total = total + r_z[k - 1].astype(jnp.float32)
        out_ref[...] = total * scale

    def finish_ax(turn_no, heads=(0, 1)):
        chains, block = ax[turn_no]
        for head in heads:
            add_into(block(x, head), [chains[head].last(), chains[3 - head].last()])

    sent_0 = attend_own(0)
    sent_1 = attend_own(1)
    for one in got_h:
        one.wait_recv()
    products(0, sent_0)
    step_all(ax[0][0], (0, 1, 2, 3))
    step_all(by, (0, 1))
    sent_2 = attend_own(2)
    products(1, sent_1)
    step_all(ax[1][0], (0, 1, 2, 3))
    sent_3 = attend_own(3)
    step_all(ax[0][0], (0, 1))
    step_all(by, (0, 2))
    products(2, sent_2)
    step_all(ax[2][0], (0, 1, 3, 2))
    step_all(by, (1, 3))
    products(3, sent_3)
    step_all(by, (0,))
    step_all(ax[1][0], (0, 1))
    step_all(ax[3][0], (0, 1))
    step_all(by, (2, 1))
    conv_next()
    step_all(by, (3,))
    finish_ax(0)
    step_all(ay, (0, 1))
    step_all(ax[2][0], (0, 1))
    step_all(ax[3][0], (2, 3))
    step_all(by, (0,))
    attend_next(0)
    step_all(by, (2, 1))
    finish_ax(1)
    step_all(ay, (0, 2))
    step_all(by, (3,))
    attend_next(1)
    step_all(ax[3][0], (0, 1))
    finish_ax(2)
    step_all(ay, (1, 3, 0, 2))
    finish_four(by, by_block, y)
    step_all(bx, (0, 1, 2, 3))
    step_all(ay, (1, 3))
    step_all(bx, (0, 1))
    finish_ax(3)
    step_all(ay, (0, 2, 1, 3))
    finish_four(bx, bx_block, x)
    finish_four(ay, ay_block, y)
    landed = send_column()
    attend_next(2)
    attend_next(3)
    spread()
    finish(landed)
    for one in sent:
        one.wait_send()


SLOTS = 112


def whole_step(frames_in, valid_frames, taps, w_qkv, cotangent):
    vmem, anywhere = pl.BlockSpec(memory_space=pltpu.VMEM), pl.BlockSpec(memory_space=pl.ANY)
    bf16, f32 = jnp.bfloat16, jnp.float32
    rows = jax.ShapeDtypeStruct((1, FRAMES, WIDTH), bf16)
    scale = float(lax.axis_size("dp") * lax.axis_size("tm") * FRAMES) ** (-0.5)
    scratch = [
        ((KERNEL, WIDTH), f32), ((FRAMES, WIDTH), bf16), ((FRAMES, WIDTH), bf16),
        ((HALO, WIDTH), bf16), ((HALO, WIDTH), bf16), ((HALO, WIDTH), bf16),
        ((EXT + 8, WIDTH), f32), ((EXT, WIDTH), bf16), ((EXT, WIDTH), f32), ((AHEAD, WIDTH), bf16),
        ((FRAMES, AHEAD), f32), ((HALO, 2 * HALO), f32),
        ((PAIRS, WIDTH, SECTION), bf16), ((PAIRS, EXT, SECTION), bf16), ((PAIRS, FRAMES, 2 * PAIR), f32),
        ((GROWS, SECTION), bf16), ((GROWS, WIDTH), f32), ((GROWS, WIDTH), f32),
        ((2, WIDTH // 2, FRAMES), bf16), ((2, WIDTH // 2, HALO), bf16),
        ((WIDTH // 2, FRAMES), bf16), ((WIDTH // 2, HALO), bf16),
        ((PAIRS, FRAMES, SECTION), bf16), ((PAIRS, HALO, 2 * PAIR), bf16),
        ((PAIRS, FRAMES, SECTION), bf16), ((PAIRS, HALO, 2 * PAIR), bf16),
        ((NX, NY, NZ_HI, ROWS_A, HEAD), bf16), ((NY, NX, NZ_HI, ROWS_B, HEAD), bf16),
        ((PAIRS, 6, NZ_HI, ROWS_A, HEAD), bf16), ((14, NX // 2, NZ_HI, ROWS_B, HEAD), bf16),
        ((14, NZ_HI // 2, ROWS_A, HEAD), bf16), ((6, NZ_HI // 2, ROWS_B, HEAD), bf16),
        ((NZ, 32, HEAD), bf16), ((NZ - 1, 32, HEAD), bf16),
    ]
    return pl.pallas_call(
        functools.partial(step_kernel, scale),
        out_shape=(rows, rows, jax.ShapeDtypeStruct((32, HEAD), f32)),
        in_specs=[pl.BlockSpec(memory_space=pltpu.SMEM)] + [anywhere] * 4,
        out_specs=(vmem, vmem, vmem),
        scratch_shapes=[pltpu.VMEM(shape, kind) for shape, kind in scratch]
        + [pltpu.SemaphoreType.DMA((3 + 3 * PAIRS,)), pltpu.SemaphoreType.DMA((SLOTS,)), pltpu.SemaphoreType.DMA((SLOTS,))],
        compiler_params=pltpu.CompilerParams(
            collective_id=0, has_side_effects=True, vmem_limit_bytes=54500 * 1024
        ),
        name="step",
    )(valid_frames, frames_in, cotangent, taps, w_qkv)


def on_device(frames_in, valid_frames, kernel, w_qkv, cotangent):
    attended, grad_in, block = whole_step(frames_in, valid_frames, kernel, w_qkv, cotangent)
    return (attended, grad_in, block.T[None])


def solution(mesh):
    return jax.shard_map(
        on_device,
        mesh=mesh,
        in_specs=(P("dp", "tm", None), P("dp"), P(), P(), P("dp", "tm", None)),
        out_specs=(P("dp", "tm", None), P("dp", "tm", None), P("dp", None, "tm")),
        check_vma=False,
    )
```

```python
import functools

import jax
import jax.numpy as jnp
from jax import lax
from jax.experimental import pallas as pl
from jax.experimental.pallas import tpu as pltpu
from jax.sharding import PartitionSpec as P

HEADS = 8
HEAD = 128
KERNEL = 9
LEFT = 70
HALO = 80
FRAMES = 128
WIDTH = 1024
EXT = HALO + FRAMES + HALO
AHEAD = FRAMES + HALO
GROWS = FRAMES + 16
PAIRS = HEADS // 2
ROWS_A, ROWS_B = 64, 32
PAIR = 2 * HEAD
SECTION = 3 * PAIR

NX, NY, NZ, NZ_LO = 4, 8, 12, 3
NZ_HI = NZ // NZ_LO
MESH = pl.DeviceIdType.MESH


def dot_nn(a, b):
    return lax.dot_general(a, b, (((1,), (0,)), ((), ())), preferred_element_type=jnp.float32)


def dot_nt(a, b):
    return lax.dot_general(a, b, (((1,), (1,)), ((), ())), preferred_element_type=jnp.float32)


def dot_tn(a, b):
    return lax.dot_general(a, b, (((0,), (0,)), ((), ())), preferred_element_type=jnp.float32)


def step_kernel(
    scale, count_ref, x_hbm, c_hbm, taps_hbm, w_hbm,
    att_out, gin_out, sum_out,
    att_ref, gin_ref, out_ref, taps_ref, x_own, c_own, xp, xn, cn, ext, hid, slope, cot, mask_own, mask_next, wbuf, qkv, near, gq, gh, gc,
    ht_own, ht_prev, hr_own, hr_prev, g_own, g_prev, gr_own, gr_prev,
    wa, wb, r_ax, r_by, r_ay, r_bx, last, r_z, local, send, recv,
):
    tm, dp = lax.axis_index("tm"), lax.axis_index("dp")
    steps = lax.axis_size("tm")
    core = lax.rem(tm, 2)
    zh = lax.rem(tm // 2, NZ_HI)
    x = tm // (2 * NZ_HI)
    y = lax.rem(dp, NY)
    zl = dp // NY
    z = zh * NZ_LO + zl
    begin = tm * FRAMES
    count = count_ref[0]
    factor = HEAD ** (-0.5)

    def device(x, y, z, core):
        return {"tm": (x * NZ_HI + z // NZ_LO) * 2 + core, "dp": lax.rem(z, NZ_LO) * NY + y}

    after, before = {"tm": lax.rem(tm + 1, steps)}, {"tm": lax.rem(tm + steps - 1, steps)}
    partner = device(x, y, z, 1 - core)
    near_by = {
        ("x", 1): device(lax.rem(x + 1, NX), y, z, core),
        ("x", -1): device(lax.rem(x + NX - 1, NX), y, z, core),
        ("y", 1): device(x, lax.rem(y + 1, NY), z, core),
        ("y", -1): device(x, lax.rem(y + NY - 1, NY), z, core),
    }
    column = [device(x, y, lax.rem(z + k, NZ), core) for k in range(1, NZ)]

    barrier = pltpu.get_barrier_semaphore()
    row = [device(lax.rem(x + k, NX), y, z, core) for k in range(1, NX)]
    peers = [after, before, *near_by.values(), row[1], *column]
    for other in peers:
        pl.semaphore_signal(barrier, inc=1, device_id=other, device_id_type=MESH)

    order = [lax.rem(y // 2 + turn, PAIRS) for turn in (2, 1, 3, 0)]

    def weight(pair, section):
        return pltpu.make_async_copy(
            w_hbm.at[:, pl.ds(section * WIDTH + pair * PAIR, PAIR)],
            wbuf.at[pair, :, pl.ds(section * PAIR, PAIR)],
            local.at[3 + pair],
        )

    pl.semaphore_wait(barrier, len(peers))

    slots = iter(range(SLOTS))
    groups = [xp, xn, cn, hr_own, hr_prev, gr_own, gr_prev, r_ax, r_by, r_ay, r_bx, r_z]

    def describe(source, target, group, slot, other):
        return pltpu.make_async_remote_copy(
            src_ref=source,
            dst_ref=target,
            send_sem=send.at[group],
            recv_sem=recv.at[slot],
            device_id=other,
            device_id_type=MESH,
        )

    def start(source, target, other, group, slot=None):
        one = describe(source, target, group, next(slots) if slot is None else slot, other)
        one.start()
        return one

    got_xp = start(x_hbm.at[0, pl.ds(FRAMES - HALO, HALO)], xp, after, 0)
    got_xn = start(x_hbm.at[0, pl.ds(0, HALO)], xn, before, 1)
    own = [
        pltpu.make_async_copy(x_hbm.at[0], x_own, local.at[0]),
        pltpu.make_async_copy(taps_hbm, taps_ref, local.at[2]),
        pltpu.make_async_copy(c_hbm.at[0], c_own, local.at[1]),
    ]
    for one in own:
        one.start()
    got_cn = start(c_hbm.at[0, pl.ds(0, HALO)], cn, before, 2)
    for pair in order:
        for section in range(3):
            weight(pair, section).start()

    def live_rows(first, rows):
        at = first + lax.broadcasted_iota(jnp.int32, (rows, 1), 0)
        return (at >= 0) & (at < count)

    def masked(first, value):
        return jnp.where(live_rows(first, value.shape[0]), value.astype(jnp.float32), 0.0)

    def band(rows, columns, first_query, first_key):
        query = first_query + lax.broadcasted_iota(jnp.int32, (rows, columns), 0)
        key = first_key + lax.broadcasted_iota(jnp.int32, (rows, columns), 1)
        offset = query - key
        allowed = (offset >= 0) & (offset <= LEFT) & (key >= 0) & (key < count) & (query < count)
        return jnp.where(allowed, 1.0, 0.0)

    def conv_rows(step, _):
        row = pl.multiple_of(step * 16, 16)
        window = ext[pl.ds(row, 24), :]
        total = jnp.zeros((16, WIDTH), jnp.float32)
        for tap in range(KERNEL):
            total = total + taps_ref[tap : tap + 1, :] * window[tap : tap + 16]
        logistic = 1.0 / (1.0 + jnp.exp(-total))
        hid[pl.ds(row, 16), :] = (window[8:24] + total * logistic).astype(jnp.bfloat16)
        slope[pl.ds(row, 16), :] = logistic * (1.0 + total * (1.0 - logistic))
        return 0

    def turn(first, take, target):
        for block in range(WIDTH // 128):
            tile = hid[first : first + FRAMES, block * 128 : (block + 1) * 128]
            turned = tile.astype(jnp.float32).T.astype(jnp.bfloat16)[:, 0:take]
            for group in range(4):
                place, side = (block * 2 + group // 2) * 32, group % 2
                target[side, place : place + 32, :] = turned[group * 32 : (group + 1) * 32]

    inner = HALO + 16
    ext[0:8, :] = jnp.zeros((8, WIDTH), jnp.float32)
    mask_own[...] = band(FRAMES, AHEAD, begin, begin - HALO)
    mask_next[...] = band(HALO, 2 * HALO, begin + FRAMES, begin + FRAMES - HALO)
    own[0].wait()
    own[1].wait()
    ext[8 + HALO : 8 + AHEAD, :] = masked(begin, x_own[...])
    lax.fori_loop(inner // 16, AHEAD // 16, conv_rows, 0)
    own[2].wait()
    cot[0:FRAMES, :] = masked(begin, c_own[...]).astype(jnp.bfloat16)
    for pair in order:
        pltpu.make_async_copy(wbuf.at[pair], wbuf.at[pair], local.at[3 + pair]).wait()
        qkv[pair, inner:AHEAD, :] = dot_nn(hid[inner:AHEAD, :], wbuf[pair]).astype(jnp.bfloat16)

    got_xp.wait_recv()
    ext[8 : 8 + HALO, :] = masked(begin - HALO, xp[...])
    lax.fori_loop(0, inner // 16, conv_rows, 0)
    turn(HALO, FRAMES, ht_own)
    turn(0, HALO, ht_prev)
    got_h = [
        start(ht_own.at[1 - core], hr_own, partner, 3),
        start(ht_prev.at[1 - core], hr_prev, partner, 4),
    ]

    def attend(q, g, k, v, mask, first):
        raised = jnp.where(mask > 0.5, jnp.exp(dot_nt(q, k) * factor), 0.0)
        at = first + lax.broadcasted_iota(jnp.int32, (q.shape[0], 1), 0)
        missing = jnp.where(at < count, 0.0, 1.0)
        prob = raised * (1.0 / (jnp.sum(raised, axis=1, keepdims=True) + missing))
        grad_prob = dot_nt(g, v)
        mean = jnp.sum(prob * grad_prob, axis=1, keepdims=True)
        grad_score = (prob * (grad_prob - mean) * factor).astype(jnp.bfloat16)
        return prob.astype(jnp.bfloat16), grad_score

    def section_at(section, head):
        return slice(section * PAIR + head * HEAD, section * PAIR + (head + 1) * HEAD)

    def lanes(pair, head):
        return pl.ds(pl.multiple_of(pair * PAIR + head * HEAD, HEAD), HEAD)

    def attend_own(turn_no):
        pair = order[turn_no]
        qkv[pair, 0:inner, :] = dot_nn(hid[0:inner, :], wbuf[pair]).astype(jnp.bfloat16)
        for head in range(2):
            q = qkv[pair, HALO:AHEAD, section_at(0, head)]
            k = qkv[pair, 0:AHEAD, section_at(1, head)]
            v = qkv[pair, 0:AHEAD, section_at(2, head)]
            g = cot[0:FRAMES, lanes(pair, head)]
            prob, score = attend(q, g, k, v, mask_own[...], begin)
            att_ref[0, :, lanes(pair, head)] = dot_nn(prob, v).astype(jnp.bfloat16)
            g_own[turn_no, :, section_at(0, head)] = dot_nn(score, k).astype(jnp.bfloat16)
            for section, left, right in ((1, score, q), (2, prob, g)):
                total = dot_tn(left, right)
                g_prev[turn_no, :, section_at(section - 1, head)] = total[0:HALO].astype(jnp.bfloat16)
                g_own[turn_no, :, section_at(section, head)] = total[HALO:AHEAD].astype(jnp.bfloat16)
                near[turn_no, :, section_at(section - 1, head)] = total[HALO:AHEAD]
        return [
            start(g_own.at[turn_no], gr_own.at[turn_no], partner, 5),
            start(g_prev.at[turn_no], gr_prev.at[turn_no], partner, 6),
        ]

    def products(turn_no, landed):
        for one in landed:
            one.wait_recv()
        pair = order[turn_no]
        for section in range(3):
            at = slice(section * PAIR, (section + 1) * PAIR)
            if section == 0:
                left = jnp.concatenate([ht_own[core], hr_own[...]], axis=1)
                right = jnp.concatenate([g_own[turn_no, :, at], gr_own[turn_no, :, at]], axis=0)
                product = dot_nn(left, right)
            else:
                low = slice((section - 1) * PAIR, section * PAIR)
                product = dot_nn(
                    jnp.concatenate([ht_own[core], ht_prev[core]], axis=1),
                    jnp.concatenate([g_own[turn_no, :, at], g_prev[turn_no, :, low]], axis=0),
                ) + dot_nn(
                    jnp.concatenate([hr_own[...], hr_prev[...]], axis=1),
                    jnp.concatenate([gr_own[turn_no, :, at], gr_prev[turn_no, :, low]], axis=0),
                )
            product = product.astype(jnp.bfloat16)
            for row in range(NX):
                for high in range(NZ_HI):
                    first = (row * NZ_HI + high) * 32
                    for head in range(2):
                        value = product[first : first + 32, head * HEAD : (head + 1) * HEAD]
                        if section == 0:
                            wa[row, pair * 2 + head, high, 0:32, :] = value
                        else:
                            at_a, at_b = 16 + section * 16, section * 16 - 16
                            wa[row, pair * 2 + head, high, at_a : at_a + 16, :] = value[0:16]
                            wb[pair * 2 + head, row, high, at_b : at_b + 16, :] = value[16:32]

    def add_into(ref, landed):
        total = ref[...].astype(jnp.float32)
        for one in landed:
            total = total + one[...].astype(jnp.float32)
        ref[...] = total.astype(jnp.bfloat16)

    class Chain:
        def __init__(self, group, axis, size, at, way, length, block, landing):
            self.group = group
            self.to, self.size, self.at, self.way, self.length = near_by[axis, way], size, at, way, length
            self.block, self.landing, self.done, self.pending = block, landing, 0, None

        def step(self):
            self.done += 1
            place = lax.rem(self.at + self.size + self.way * (self.length - self.done + 1), self.size)
            ref = self.block(place)
            if self.pending is not None:
                self.pending.wait_recv()
                add_into(ref, [self.landing(self.done - 2)])
            self.pending = start(ref, self.landing(self.done - 1), self.to, self.group)

        def last(self):
            self.pending.wait_recv()
            return self.landing(self.length - 1)

    def half(ref, which, size):
        return ref.at[pl.ds(which * (size // 2), size // 2)]

    def four(group, axis, size, at, block, landing):
        far, less = size // 2, size // 2 - 1
        chains, slot = [], 0
        for way, which, length in ((1, 0, far), (-1, 1, far), (1, 1, less), (-1, 0, less)):
            chains.append(
                Chain(group, axis, size, at, way, length,
                      lambda place, which=which: block(place, which),
                      lambda step, slot=slot: landing.at[slot + step])
            )
            slot += length
        return chains

    def finish_four(chains, block, at):
        add_into(block(at, 0), [chains[0].last(), chains[3].last()])
        add_into(block(at, 1), [chains[1].last(), chains[2].last()])

    ax = []
    for turn_no in range(PAIRS):
        def head_block(place, which, turn_no=turn_no):
            return wa.at[place, order[turn_no] * 2 + which]
        ax.append((four(7, "x", NX, x, head_block, r_ax.at[turn_no]), head_block))

    def by_block(place, which):
        return half(wb.at[place], which, NX)

    def ay_block(place, which):
        return half(wa.at[x, place], which, NZ_HI)

    by = four(8, "y", NY, y, by_block, r_by)
    ay = four(9, "y", NY, y, ay_block, r_ay)

    def step_all(chains, which):
        for index in which:
            chains[index].step()

    def attend_next(turn_no):
        pair = order[turn_no]
        qkv[pair, AHEAD:EXT, :] = dot_nn(hid[AHEAD:EXT, :], wbuf[pair]).astype(jnp.bfloat16)
        gq[0:FRAMES, 0:PAIR] = g_own[turn_no, :, 0:PAIR]
        for head in range(2):
            q = qkv[pair, AHEAD:EXT, section_at(0, head)]
            k = qkv[pair, FRAMES:EXT, section_at(1, head)]
            v = qkv[pair, FRAMES:EXT, section_at(2, head)]
            g = cot[FRAMES:AHEAD, lanes(pair, head)]
            prob, score = attend(q, g, k, v, mask_next[...], begin + FRAMES)
            gq[FRAMES:GROWS, section_at(0, head)] = dot_nn(score[0:16], k).astype(jnp.bfloat16)
            split = FRAMES - HALO
            for section, left, right in ((1, score, q), (2, prob, g)):
                far = dot_tn(left, right)
                at = section_at(section, head)
                mine = near.at[turn_no, :, section_at(section - 1, head)]
                gq[0:split, at] = mine[0:split].astype(jnp.bfloat16)
                gq[split:FRAMES, at] = (mine[split:FRAMES] + far[0:HALO]).astype(jnp.bfloat16)
                gq[FRAMES:GROWS, at] = far[HALO : HALO + 16].astype(jnp.bfloat16)
        gh[...] += dot_nt(gq[...], wbuf[pair])

    def conv_next():
        got_xn.wait_recv()
        ext[8 + AHEAD : 8 + EXT, :] = masked(begin + FRAMES, xn[...])
        lax.fori_loop(AHEAD // 16, EXT // 16, conv_rows, 0)
        got_cn.wait_recv()
        cot[FRAMES:AHEAD, :] = masked(begin + FRAMES, cn[...]).astype(jnp.bfloat16)
        gh[...] = jnp.zeros_like(gh)

    def spread_rows(step, _):
        row = pl.multiple_of(step * 16, 16)
        total = gh[pl.ds(row, 16), :]
        window = gc[pl.ds(row, 24), :]
        for tap in range(KERNEL):
            total = total + taps_ref[tap : tap + 1, :] * window[8 - tap : 24 - tap]
        gin_ref[0, pl.ds(row, 16), :] = jnp.where(live_rows(begin + row, 16), total, 0.0).astype(jnp.bfloat16)
        return 0

    def spread():
        gc[...] = gh[...] * slope[HALO : HALO + GROWS, :]
        lax.fori_loop(0, FRAMES // 16, spread_rows, 0)

    def send_row():
        for k in (2, 1, 3):
            start(wb.at[y, lax.rem(x + k, NX)], r_bx.at[k - 1], row[k - 1], 10, SLOTS)

    def finish_row():
        describe(r_bx, r_bx, 10, SLOTS, partner).wait_recv()
        add_into(wb.at[y, x], [r_bx.at[k] for k in range(NX - 1)])

    def send_column():
        for high in range(NZ_HI):
            last[high * NZ_LO] = wa[x, y, high, 0:32, :]
            for section in range(1, NZ_LO):
                at_a, at_b = 16 + section * 16, section * 16 - 16
                last[high * NZ_LO + section, 0:16, :] = wa[x, y, high, at_a : at_a + 16, :]
                last[high * NZ_LO + section, 16:32, :] = wb[y, x, high, at_b : at_b + 16, :]
        far_first = sorted(range(1, NZ), key=lambda k: abs(k - NZ // 2))
        for k in far_first:
            start(last.at[lax.rem(z + k, NZ)], r_z.at[k - 1], column[k - 1], 11, SLOTS + 1)

    def finish():
        describe(r_z, r_z, 11, SLOTS + 1, partner).wait_recv()
        total = last[z].astype(jnp.float32)
        for k in range(NZ - 1):
            total = total + r_z[k].astype(jnp.float32)
        out_ref[...] = total * scale

    def finish_ax(turn_no, heads=(0, 1)):
        chains, block = ax[turn_no]
        for head in heads:
            add_into(block(x, head), [chains[head].last(), chains[3 - head].last()])

    sent_0 = attend_own(0)
    sent_1 = attend_own(1)
    for one in got_h:
        one.wait_recv()
    products(0, sent_0)
    step_all(ax[0][0], (0, 1, 2, 3))
    step_all(by, (0, 1))
    sent_2 = attend_own(2)
    products(1, sent_1)
    step_all(ax[1][0], (0, 1, 2, 3))
    sent_3 = attend_own(3)
    results = [pltpu.make_async_copy(att_ref, att_out, local.at[3 + PAIRS])]
    results[0].start()
    step_all(ax[0][0], (0, 1))
    step_all(by, (0, 2))
    products(2, sent_2)
    step_all(ax[2][0], (0, 1))
    step_all(by, (1, 3))
    products(3, sent_3)
    step_all(ax[1][0], (0, 1))
    step_all(ax[2][0], (3, 2))
    step_all(by, (0, 2, 1))
    conv_next()
    finish_ax(0)
    step_all(ay, (0, 1))
    step_all(ax[2][0], (0, 1))
    step_all(ax[3][0], (0, 1, 3, 2))
    step_all(by, (3, 0))
    attend_next(0)
    finish_ax(1)
    step_all(ay, (0, 2))
    step_all(by, (2, 1, 3))
    finish_ax(2)
    step_all(ay, (1, 3))
    step_all(ax[3][0], (0, 1))
    step_all(ay, (0, 2))
    finish_four(by, by_block, y)
    send_row()
    step_all(ay, (1, 3))
    finish_ax(3)
    step_all(ay, (0, 2, 1, 3))
    finish_row()
    finish_four(ay, ay_block, y)
    send_column()
    attend_next(1)
    attend_next(2)
    attend_next(3)
    spread()
    results.append(pltpu.make_async_copy(gin_ref, gin_out, local.at[4 + PAIRS]))
    results[1].start()
    finish()
    results.append(pltpu.make_async_copy(out_ref, sum_out, local.at[5 + PAIRS]))
    results[2].start()
    for one in results:
        one.wait()
    for group, whole in enumerate(groups):
        describe(whole, whole, group, 0, partner).wait_send()


SLOTS = 65


def whole_step(frames_in, valid_frames, taps, w_qkv, cotangent):
    anywhere = pl.BlockSpec(memory_space=pl.ANY)
    bf16, f32 = jnp.bfloat16, jnp.float32
    rows = jax.ShapeDtypeStruct((1, FRAMES, WIDTH), bf16)
    scale = float(lax.axis_size("dp") * lax.axis_size("tm") * FRAMES) ** (-0.5)
    scratch = [
        ((1, FRAMES, WIDTH), bf16), ((1, FRAMES, WIDTH), bf16), ((32, HEAD), f32),
        ((KERNEL, WIDTH), f32), ((FRAMES, WIDTH), bf16), ((FRAMES, WIDTH), bf16),
        ((HALO, WIDTH), bf16), ((HALO, WIDTH), bf16), ((HALO, WIDTH), bf16),
        ((EXT + 8, WIDTH), f32), ((EXT, WIDTH), bf16), ((EXT, WIDTH), f32), ((AHEAD, WIDTH), bf16),
        ((FRAMES, AHEAD), f32), ((HALO, 2 * HALO), f32),
        ((PAIRS, WIDTH, SECTION), bf16), ((PAIRS, EXT, SECTION), bf16), ((PAIRS, FRAMES, 2 * PAIR), f32),
        ((GROWS, SECTION), bf16), ((GROWS, WIDTH), f32), ((GROWS, WIDTH), f32),
        ((2, WIDTH // 2, FRAMES), bf16), ((2, WIDTH // 2, HALO), bf16),
        ((WIDTH // 2, FRAMES), bf16), ((WIDTH // 2, HALO), bf16),
        ((PAIRS, FRAMES, SECTION), bf16), ((PAIRS, HALO, 2 * PAIR), bf16),
        ((PAIRS, FRAMES, SECTION), bf16), ((PAIRS, HALO, 2 * PAIR), bf16),
        ((NX, NY, NZ_HI, ROWS_A, HEAD), bf16), ((NY, NX, NZ_HI, ROWS_B, HEAD), bf16),
        ((PAIRS, 6, NZ_HI, ROWS_A, HEAD), bf16), ((14, NX // 2, NZ_HI, ROWS_B, HEAD), bf16),
        ((14, NZ_HI // 2, ROWS_A, HEAD), bf16), ((NX - 1, NZ_HI, ROWS_B, HEAD), bf16),
        ((NZ, 32, HEAD), bf16), ((NZ - 1, 32, HEAD), bf16),
    ]
    return pl.pallas_call(
        functools.partial(step_kernel, scale),
        out_shape=(rows, rows, jax.ShapeDtypeStruct((32, HEAD), f32)),
        in_specs=[pl.BlockSpec(memory_space=pltpu.SMEM)] + [anywhere] * 4,
        out_specs=(anywhere,) * 3,
        scratch_shapes=[pltpu.VMEM(shape, kind) for shape, kind in scratch]
        + [pltpu.SemaphoreType.DMA((6 + PAIRS,)), pltpu.SemaphoreType.DMA((12,)), pltpu.SemaphoreType.DMA((SLOTS + 2,))],
        compiler_params=pltpu.CompilerParams(
            collective_id=0, has_side_effects=True, vmem_limit_bytes=54500 * 1024
        ),
        name="step",
    )(valid_frames, frames_in, cotangent, taps, w_qkv)


def on_device(frames_in, valid_frames, kernel, w_qkv, cotangent):
    attended, grad_in, block = whole_step(frames_in, valid_frames, kernel, w_qkv, cotangent)
    return (attended, grad_in, block.T[None])


def solution(mesh):
    return jax.shard_map(
        on_device,
        mesh=mesh,
        in_specs=(P("dp", "tm", None), P("dp"), P(), P(), P("dp", "tm", None)),
        out_specs=(P("dp", "tm", None), P("dp", "tm", None), P("dp", None, "tm")),
        check_vma=False,
    )
```

```python
import functools

import jax
import jax.numpy as jnp
from jax import lax
from jax.experimental import pallas as pl
from jax.experimental.pallas import tpu as pltpu
from jax.sharding import PartitionSpec as P

HEADS = 8
HEAD = 128
KERNEL = 9
LEFT = 70
HALO = 80
FRAMES = 128
WIDTH = 1024
EXT = HALO + FRAMES + HALO
AHEAD = FRAMES + HALO
GROWS = FRAMES + 16
PAIRS = HEADS // 2
ROWS_A, ROWS_B = 56, 40
PLACES = ((0, 0, 24), (24, 8, 16), (40, 24, 16))
PAIR = 2 * HEAD
SECTION = 3 * PAIR

NX, NY, NZ, NZ_LO = 4, 8, 12, 3
NZ_HI = NZ // NZ_LO
MESH = pl.DeviceIdType.MESH


def dot_nn(a, b):
    return lax.dot_general(a, b, (((1,), (0,)), ((), ())), preferred_element_type=jnp.float32)


def dot_nt(a, b):
    return lax.dot_general(a, b, (((1,), (1,)), ((), ())), preferred_element_type=jnp.float32)


def dot_tn(a, b):
    return lax.dot_general(a, b, (((0,), (0,)), ((), ())), preferred_element_type=jnp.float32)


def step_kernel(
    scale, count_ref, x_hbm, c_hbm, taps_hbm, w_hbm,
    att_out, gin_out, sum_out,
    att_ref, gin_ref, out_ref, taps_ref, x_own, c_own, xp, xn, cn, ext, hid, slope, cot, mask_own, mask_next, wbuf, qkv, near, gq, gh, gc,
    ht_own, ht_prev, hr_own, hr_prev, g_own, g_prev, gr_own, gr_prev,
    wa, wb, r_ax, r_by, r_ay, r_bx, last, r_z, local, send, recv,
):
    tm, dp = lax.axis_index("tm"), lax.axis_index("dp")
    steps = lax.axis_size("tm")
    core = lax.rem(tm, 2)
    zh = lax.rem(tm // 2, NZ_HI)
    x = tm // (2 * NZ_HI)
    y = lax.rem(dp, NY)
    zl = dp // NY
    z = zh * NZ_LO + zl
    begin = tm * FRAMES
    count = count_ref[0]
    factor = HEAD ** (-0.5)

    def device(x, y, z, core):
        return {"tm": (x * NZ_HI + z // NZ_LO) * 2 + core, "dp": lax.rem(z, NZ_LO) * NY + y}

    after, before = {"tm": lax.rem(tm + 1, steps)}, {"tm": lax.rem(tm + steps - 1, steps)}
    partner = device(x, y, z, 1 - core)
    near_by = {
        ("x", 1): device(lax.rem(x + 1, NX), y, z, core),
        ("x", -1): device(lax.rem(x + NX - 1, NX), y, z, core),
        ("y", 1): device(x, lax.rem(y + 1, NY), z, core),
        ("y", -1): device(x, lax.rem(y + NY - 1, NY), z, core),
    }
    column = [device(x, y, lax.rem(z + k, NZ), core) for k in range(1, NZ)]

    barrier = pltpu.get_barrier_semaphore()
    row = [device(lax.rem(x + k, NX), y, z, core) for k in range(1, NX)]
    peers = [after, before, *near_by.values(), row[1], *column]
    for other in peers:
        pl.semaphore_signal(barrier, inc=1, device_id=other, device_id_type=MESH)

    order = [lax.rem(y // 2 + turn, PAIRS) for turn in (2, 1, 3, 0)]

    def weight(pair, section):
        return pltpu.make_async_copy(
            w_hbm.at[:, pl.ds(section * WIDTH + pair * PAIR, PAIR)],
            wbuf.at[pair, :, pl.ds(section * PAIR, PAIR)],
            local.at[3 + pair],
        )

    pl.semaphore_wait(barrier, len(peers))

    slots = iter(range(SLOTS))
    groups = [xp, xn, cn, hr_own, hr_prev, gr_own, gr_prev, r_ax, r_by, r_ay, r_bx, r_z]

    def describe(source, target, group, slot, other):
        return pltpu.make_async_remote_copy(
            src_ref=source,
            dst_ref=target,
            send_sem=send.at[group],
            recv_sem=recv.at[slot],
            device_id=other,
            device_id_type=MESH,
        )

    def start(source, target, other, group, slot=None):
        one = describe(source, target, group, next(slots) if slot is None else slot, other)
        one.start()
        return one

    got_xp = start(x_hbm.at[0, pl.ds(FRAMES - HALO, HALO)], xp, after, 0)
    got_xn = start(x_hbm.at[0, pl.ds(0, HALO)], xn, before, 1)
    own = [
        pltpu.make_async_copy(x_hbm.at[0], x_own, local.at[0]),
        pltpu.make_async_copy(taps_hbm, taps_ref, local.at[2]),
        pltpu.make_async_copy(c_hbm.at[0], c_own, local.at[1]),
    ]
    for one in own:
        one.start()
    got_cn = start(c_hbm.at[0, pl.ds(0, HALO)], cn, before, 2)
    for pair in order:
        for section in range(3):
            weight(pair, section).start()

    def live_rows(first, rows):
        at = first + lax.broadcasted_iota(jnp.int32, (rows, 1), 0)
        return (at >= 0) & (at < count)

    def masked(first, value):
        return jnp.where(live_rows(first, value.shape[0]), value.astype(jnp.float32), 0.0)

    def band(rows, columns, first_query, first_key):
        query = first_query + lax.broadcasted_iota(jnp.int32, (rows, columns), 0)
        key = first_key + lax.broadcasted_iota(jnp.int32, (rows, columns), 1)
        offset = query - key
        allowed = (offset >= 0) & (offset <= LEFT) & (key >= 0) & (key < count) & (query < count)
        return jnp.where(allowed, 1.0, 0.0)

    def conv_rows(step, _):
        row = pl.multiple_of(step * 16, 16)
        window = ext[pl.ds(row, 24), :]
        total = jnp.zeros((16, WIDTH), jnp.float32)
        for tap in range(KERNEL):
            total = total + taps_ref[tap : tap + 1, :] * window[tap : tap + 16]
        logistic = 1.0 / (1.0 + jnp.exp(-total))
        hid[pl.ds(row, 16), :] = (window[8:24] + total * logistic).astype(jnp.bfloat16)
        slope[pl.ds(row, 16), :] = logistic * (1.0 + total * (1.0 - logistic))
        return 0

    def turn(first, take, target):
        for block in range(WIDTH // 128):
            tile = hid[first : first + FRAMES, block * 128 : (block + 1) * 128]
            turned = tile.astype(jnp.float32).T.astype(jnp.bfloat16)[:, 0:take]
            for group in range(4):
                place, side = (block * 2 + group // 2) * 32, group % 2
                target[side, place : place + 32, :] = turned[group * 32 : (group + 1) * 32]

    inner = HALO + 16
    ext[0:8, :] = jnp.zeros((8, WIDTH), jnp.float32)
    mask_own[...] = band(FRAMES, AHEAD, begin, begin - HALO)
    mask_next[...] = band(HALO, 2 * HALO, begin + FRAMES, begin + FRAMES - HALO)
    own[0].wait()
    own[1].wait()
    ext[8 + HALO : 8 + AHEAD, :] = masked(begin, x_own[...])
    lax.fori_loop(inner // 16, AHEAD // 16, conv_rows, 0)
    own[2].wait()
    cot[0:FRAMES, :] = masked(begin, c_own[...]).astype(jnp.bfloat16)
    for pair in order:
        pltpu.make_async_copy(wbuf.at[pair], wbuf.at[pair], local.at[3 + pair]).wait()
        qkv[pair, inner:AHEAD, :] = dot_nn(hid[inner:AHEAD, :], wbuf[pair]).astype(jnp.bfloat16)

    got_xp.wait_recv()
    ext[8 : 8 + HALO, :] = masked(begin - HALO, xp[...])
    lax.fori_loop(0, inner // 16, conv_rows, 0)
    turn(HALO, FRAMES, ht_own)
    turn(0, HALO, ht_prev)
    got_h = [
        start(ht_own.at[1 - core], hr_own, partner, 3),
        start(ht_prev.at[1 - core], hr_prev, partner, 4),
    ]

    def attend(q, g, k, v, mask, first):
        raised = jnp.where(mask > 0.5, jnp.exp(dot_nt(q, k) * factor), 0.0)
        at = first + lax.broadcasted_iota(jnp.int32, (q.shape[0], 1), 0)
        missing = jnp.where(at < count, 0.0, 1.0)
        prob = raised * (1.0 / (jnp.sum(raised, axis=1, keepdims=True) + missing))
        grad_prob = dot_nt(g, v)
        mean = jnp.sum(prob * grad_prob, axis=1, keepdims=True)
        grad_score = (prob * (grad_prob - mean) * factor).astype(jnp.bfloat16)
        return prob.astype(jnp.bfloat16), grad_score

    def section_at(section, head):
        return slice(section * PAIR + head * HEAD, section * PAIR + (head + 1) * HEAD)

    def lanes(pair, head):
        return pl.ds(pl.multiple_of(pair * PAIR + head * HEAD, HEAD), HEAD)

    def attend_own(turn_no):
        pair = order[turn_no]
        qkv[pair, 0:inner, :] = dot_nn(hid[0:inner, :], wbuf[pair]).astype(jnp.bfloat16)
        for head in range(2):
            q = qkv[pair, HALO:AHEAD, section_at(0, head)]
            k = qkv[pair, 0:AHEAD, section_at(1, head)]
            v = qkv[pair, 0:AHEAD, section_at(2, head)]
            g = cot[0:FRAMES, lanes(pair, head)]
            prob, score = attend(q, g, k, v, mask_own[...], begin)
            att_ref[0, :, lanes(pair, head)] = dot_nn(prob, v).astype(jnp.bfloat16)
            g_own[turn_no, :, section_at(0, head)] = dot_nn(score, k).astype(jnp.bfloat16)
            for section, left, right in ((1, score, q), (2, prob, g)):
                total = dot_tn(left, right)
                g_prev[turn_no, :, section_at(section - 1, head)] = total[0:HALO].astype(jnp.bfloat16)
                g_own[turn_no, :, section_at(section, head)] = total[HALO:AHEAD].astype(jnp.bfloat16)
                near[turn_no, :, section_at(section - 1, head)] = total[HALO:AHEAD]
        return [
            start(g_own.at[turn_no], gr_own.at[turn_no], partner, 5),
            start(g_prev.at[turn_no], gr_prev.at[turn_no], partner, 6),
        ]

    def products(turn_no, landed):
        for one in landed:
            one.wait_recv()
        pair = order[turn_no]
        for section in range(3):
            at = slice(section * PAIR, (section + 1) * PAIR)
            if section == 0:
                left = jnp.concatenate([ht_own[core], hr_own[...]], axis=1)
                right = jnp.concatenate([g_own[turn_no, :, at], gr_own[turn_no, :, at]], axis=0)
                product = dot_nn(left, right)
            else:
                low = slice((section - 1) * PAIR, section * PAIR)
                product = dot_nn(
                    jnp.concatenate([ht_own[core], ht_prev[core]], axis=1),
                    jnp.concatenate([g_own[turn_no, :, at], g_prev[turn_no, :, low]], axis=0),
                ) + dot_nn(
                    jnp.concatenate([hr_own[...], hr_prev[...]], axis=1),
                    jnp.concatenate([gr_own[turn_no, :, at], gr_prev[turn_no, :, low]], axis=0),
                )
            for row in range(NX):
                for high in range(NZ_HI):
                    first = (row * NZ_HI + high) * 32
                    for head in range(2):
                        value = product[first : first + 32, head * HEAD : (head + 1) * HEAD]
                        at_a, at_b, cut = PLACES[section]
                        wa[row, pair * 2 + head, high, at_a : at_a + cut, :] = value[0:cut].astype(jnp.bfloat16)
                        wb[pair * 2 + head, row, high, at_b : at_b + 32 - cut, :] = value[cut:32].astype(jnp.bfloat16)

    def add_into(ref, landed):
        total = ref[...].astype(jnp.float32)
        for one in landed:
            total = total + one[...].astype(jnp.float32)
        ref[...] = total.astype(jnp.bfloat16)

    class Chain:
        def __init__(self, group, axis, size, at, way, length, block, landing):
            self.group = group
            self.to, self.size, self.at, self.way, self.length = near_by[axis, way], size, at, way, length
            self.block, self.landing, self.done, self.pending = block, landing, 0, None

        def step(self):
            self.done += 1
            place = lax.rem(self.at + self.size + self.way * (self.length - self.done + 1), self.size)
            ref = self.block(place)
            if self.pending is not None:
                self.pending.wait_recv()
                add_into(ref, [self.landing(self.done - 2)])
            self.pending = start(ref, self.landing(self.done - 1), self.to, self.group)

        def last(self):
            self.pending.wait_recv()
            return self.landing(self.length - 1)

    def half(ref, which, size):
        return ref.at[pl.ds(which * (size // 2), size // 2)]

    def four(group, axis, size, at, block, landing):
        far, less = size // 2, size // 2 - 1
        chains, slot = [], 0
        for way, which, length in ((1, 0, far), (-1, 1, far), (1, 1, less), (-1, 0, less)):
            chains.append(
                Chain(group, axis, size, at, way, length,
                      lambda place, which=which: block(place, which),
                      lambda step, slot=slot: landing.at[slot + step])
            )
            slot += length
        return chains

    def finish_four(chains, block, at):
        add_into(block(at, 0), [chains[0].last(), chains[3].last()])
        add_into(block(at, 1), [chains[1].last(), chains[2].last()])

    ax = []
    for turn_no in range(PAIRS):
        def head_block(place, which, turn_no=turn_no):
            return wa.at[place, order[turn_no] * 2 + which]
        ax.append((four(7, "x", NX, x, head_block, r_ax.at[turn_no]), head_block))

    def by_block(place, which):
        return half(wb.at[place], which, NX)

    def ay_block(place, which):
        return half(wa.at[x, place], which, NZ_HI)

    by = four(8, "y", NY, y, by_block, r_by)
    ay = four(9, "y", NY, y, ay_block, r_ay)

    def step_all(chains, which):
        for index in which:
            chains[index].step()

    def attend_next(turn_no):
        pair = order[turn_no]
        qkv[pair, AHEAD:EXT, :] = dot_nn(hid[AHEAD:EXT, :], wbuf[pair]).astype(jnp.bfloat16)
        gq[0:FRAMES, 0:PAIR] = g_own[turn_no, :, 0:PAIR]
        for head in range(2):
            q = qkv[pair, AHEAD:EXT, section_at(0, head)]
            k = qkv[pair, FRAMES:EXT, section_at(1, head)]
            v = qkv[pair, FRAMES:EXT, section_at(2, head)]
            g = cot[FRAMES:AHEAD, lanes(pair, head)]
            prob, score = attend(q, g, k, v, mask_next[...], begin + FRAMES)
            gq[FRAMES:GROWS, section_at(0, head)] = dot_nn(score[0:16], k).astype(jnp.bfloat16)
            split = FRAMES - HALO
            for section, left, right in ((1, score, q), (2, prob, g)):
                far = dot_tn(left, right)
                at = section_at(section, head)
                mine = near.at[turn_no, :, section_at(section - 1, head)]
                gq[0:split, at] = mine[0:split].astype(jnp.bfloat16)
                gq[split:FRAMES, at] = (mine[split:FRAMES] + far[0:HALO]).astype(jnp.bfloat16)
                gq[FRAMES:GROWS, at] = far[HALO : HALO + 16].astype(jnp.bfloat16)
        gh[...] += dot_nt(gq[...], wbuf[pair])

    def conv_next():
        got_xn.wait_recv()
        ext[8 + AHEAD : 8 + EXT, :] = masked(begin + FRAMES, xn[...])
        lax.fori_loop(AHEAD // 16, EXT // 16, conv_rows, 0)
        got_cn.wait_recv()
        cot[FRAMES:AHEAD, :] = masked(begin + FRAMES, cn[...]).astype(jnp.bfloat16)
        gh[...] = jnp.zeros_like(gh)

    def spread_rows(step, _):
        row = pl.multiple_of(step * 16, 16)
        total = gh[pl.ds(row, 16), :]
        window = gc[pl.ds(row, 24), :]
        for tap in range(KERNEL):
            total = total + taps_ref[tap : tap + 1, :] * window[8 - tap : 24 - tap]
        gin_ref[0, pl.ds(row, 16), :] = jnp.where(live_rows(begin + row, 16), total, 0.0).astype(jnp.bfloat16)
        return 0

    def spread():
        gc[...] = gh[...] * slope[HALO : HALO + GROWS, :]
        lax.fori_loop(0, FRAMES // 16, spread_rows, 0)

    def send_row():
        for k in (2, 1, 3):
            start(wb.at[y, lax.rem(x + k, NX)], r_bx.at[k - 1], row[k - 1], 10, SLOTS)

    def finish_row():
        describe(r_bx, r_bx, 10, SLOTS, partner).wait_recv()
        add_into(wb.at[y, x], [r_bx.at[k] for k in range(NX - 1)])

    def send_column():
        for high in range(NZ_HI):
            for section, (at_a, at_b, cut) in enumerate(PLACES):
                last[high * NZ_LO + section, 0:cut, :] = wa[x, y, high, at_a : at_a + cut, :]
                last[high * NZ_LO + section, cut:32, :] = wb[y, x, high, at_b : at_b + 32 - cut, :]
        far_first = sorted(range(1, NZ), key=lambda k: abs(k - NZ // 2))
        for k in far_first:
            start(last.at[lax.rem(z + k, NZ)], r_z.at[k - 1], column[k - 1], 11, SLOTS + 1)

    def finish():
        describe(r_z, r_z, 11, SLOTS + 1, partner).wait_recv()
        total = last[z].astype(jnp.float32)
        for k in range(NZ - 1):
            total = total + r_z[k].astype(jnp.float32)
        out_ref[...] = total * scale

    def finish_ax(turn_no, heads=(0, 1)):
        chains, block = ax[turn_no]
        for head in heads:
            add_into(block(x, head), [chains[head].last(), chains[3 - head].last()])

    sent_0 = attend_own(0)
    sent_1 = attend_own(1)
    for one in got_h:
        one.wait_recv()
    products(0, sent_0)
    step_all(ax[0][0], (0, 1, 2, 3))
    step_all(by, (0, 1))
    sent_2 = attend_own(2)
    products(1, sent_1)
    step_all(ax[1][0], (0, 1, 2, 3))
    step_all(by, (2,))
    sent_3 = attend_own(3)
    results = [pltpu.make_async_copy(att_ref, att_out, local.at[3 + PAIRS])]
    results[0].start()
    step_all(ax[0][0], (0, 1))
    step_all(by, (0,))
    products(2, sent_2)
    step_all(ax[2][0], (0, 1))
    step_all(by, (1, 3))
    products(3, sent_3)
    step_all(ax[1][0], (0, 1))
    step_all(ax[2][0], (3, 2))
    step_all(by, (2,))
    conv_next()
    step_all(by, (0, 1))
    finish_ax(0)
    step_all(ay, (0, 1))
    step_all(ax[2][0], (0, 1))
    step_all(ax[3][0], (0, 1, 3, 2))
    step_all(by, (3, 2))
    attend_next(0)
    step_all(by, (0, 1))
    finish_ax(1)
    step_all(ay, (0, 2))
    finish_ax(2)
    step_all(ay, (1, 3))
    step_all(by, (3,))
    step_all(ax[3][0], (0, 1))
    step_all(ay, (0, 2, 1, 3))
    finish_four(by, by_block, y)
    send_row()
    finish_ax(3)
    step_all(ay, (0, 2, 1, 3))
    finish_row()
    finish_four(ay, ay_block, y)
    send_column()
    attend_next(1)
    attend_next(2)
    attend_next(3)
    spread()
    results.append(pltpu.make_async_copy(gin_ref, gin_out, local.at[4 + PAIRS]))
    results[1].start()
    finish()
    results.append(pltpu.make_async_copy(out_ref, sum_out, local.at[5 + PAIRS]))
    results[2].start()
    for one in results:
        one.wait()
    for group, whole in enumerate(groups):
        describe(whole, whole, group, 0, partner).wait_send()


SLOTS = 65


def whole_step(frames_in, valid_frames, taps, w_qkv, cotangent):
    anywhere = pl.BlockSpec(memory_space=pl.ANY)
    bf16, f32 = jnp.bfloat16, jnp.float32
    rows = jax.ShapeDtypeStruct((1, FRAMES, WIDTH), bf16)
    scale = float(lax.axis_size("dp") * lax.axis_size("tm") * FRAMES) ** (-0.5)
    scratch = [
        ((1, FRAMES, WIDTH), bf16), ((1, FRAMES, WIDTH), bf16), ((32, HEAD), f32),
        ((KERNEL, WIDTH), f32), ((FRAMES, WIDTH), bf16), ((FRAMES, WIDTH), bf16),
        ((HALO, WIDTH), bf16), ((HALO, WIDTH), bf16), ((HALO, WIDTH), bf16),
        ((EXT + 8, WIDTH), f32), ((EXT, WIDTH), bf16), ((EXT, WIDTH), f32), ((AHEAD, WIDTH), bf16),
        ((FRAMES, AHEAD), f32), ((HALO, 2 * HALO), f32),
        ((PAIRS, WIDTH, SECTION), bf16), ((PAIRS, EXT, SECTION), bf16), ((PAIRS, FRAMES, 2 * PAIR), f32),
        ((GROWS, SECTION), bf16), ((GROWS, WIDTH), f32), ((GROWS, WIDTH), f32),
        ((2, WIDTH // 2, FRAMES), bf16), ((2, WIDTH // 2, HALO), bf16),
        ((WIDTH // 2, FRAMES), bf16), ((WIDTH // 2, HALO), bf16),
        ((PAIRS, FRAMES, SECTION), bf16), ((PAIRS, HALO, 2 * PAIR), bf16),
        ((PAIRS, FRAMES, SECTION), bf16), ((PAIRS, HALO, 2 * PAIR), bf16),
        ((NX, NY, NZ_HI, ROWS_A, HEAD), bf16), ((NY, NX, NZ_HI, ROWS_B, HEAD), bf16),
        ((PAIRS, 6, NZ_HI, ROWS_A, HEAD), bf16), ((14, NX // 2, NZ_HI, ROWS_B, HEAD), bf16),
        ((14, NZ_HI // 2, ROWS_A, HEAD), bf16), ((NX - 1, NZ_HI, ROWS_B, HEAD), bf16),
        ((NZ, 32, HEAD), bf16), ((NZ - 1, 32, HEAD), bf16),
    ]
    return pl.pallas_call(
        functools.partial(step_kernel, scale),
        out_shape=(rows, rows, jax.ShapeDtypeStruct((32, HEAD), f32)),
        in_specs=[pl.BlockSpec(memory_space=pltpu.SMEM)] + [anywhere] * 4,
        out_specs=(anywhere,) * 3,
        scratch_shapes=[pltpu.VMEM(shape, kind) for shape, kind in scratch]
        + [pltpu.SemaphoreType.DMA((6 + PAIRS,)), pltpu.SemaphoreType.DMA((12,)), pltpu.SemaphoreType.DMA((SLOTS + 2,))],
        compiler_params=pltpu.CompilerParams(
            collective_id=0, has_side_effects=True, vmem_limit_bytes=54500 * 1024
        ),
        name="step",
    )(valid_frames, *(pltpu.with_memory_space_constraint(one, pltpu.HBM) for one in (frames_in, cotangent, taps, w_qkv)))


def on_device(frames_in, valid_frames, kernel, w_qkv, cotangent):
    attended, grad_in, block = whole_step(frames_in, valid_frames, kernel, w_qkv, cotangent)
    return (attended, grad_in, block.T[None])


def solution(mesh):
    return jax.shard_map(
        on_device,
        mesh=mesh,
        in_specs=(P("dp", "tm", None), P("dp"), P(), P(), P("dp", "tm", None)),
        out_specs=(P("dp", "tm", None), P("dp", "tm", None), P("dp", None, "tm")),
        check_vma=False,
    )
```
